512 devices in a mesh: rows: 32 (over x, y, core), cols: 16 (over z).
Axes of the slice: x: 4, y: 4, z: 16, core: 2. Of those that a mesh axis runs over, the one named last changes fastest.
Arguments:
- coadd_flux: float32 [4096, 16384], P('rows', 'cols'), may hold values from -8 to 8
- inverse_variance: float32 [4096, 16384], P('rows', 'cols'), may hold values from 0.25 to 4
- source_mask: int32 [4096, 16384], P('rows', 'cols'), may hold values 0 or 1
Outputs:
- background: float32 [4096, 16384], P('rows', 'cols')
- rms_map: float32 [4096, 16384], P('rows', 'cols')
The draws below stay inside these ranges and needn't reach their ends.
All inputs are finite; a program needn't handle non-finite values. No bound on the sum of `source_mask` on one device may be relied on, other than what follows from the above.
Results may differ from the reference program's by a relative error of at most 0.0001.
Values sent between devices are 32-bit elements; how exact they have to be, the bound alone decides.
A program may use at most 64 MiB of HBM per device.

```python
import math
import jax
import jax.numpy as jnp

ITERS = 2
RADIUS = 32
NR = 4096
NC = 16384


def with_ends(entries, key, smallest, largest):
    index_at = [jax.random.randint(jax.random.fold_in(key, axis), (), 0, length) for axis, length in enumerate(entries.shape)]
    widest = entries.shape.index(max(entries.shape))
    neighbour = index_at[:widest] + [(index_at[widest] + 1) % entries.shape[widest]] + index_at[widest + 1:]
    return entries.at[tuple(index_at)].set(smallest).at[tuple(neighbour)].set(largest)


def block_scale(stream_key, shape, cuts, low, high):
    def one(dim, blocks):
        heights = jax.random.uniform(jax.random.fold_in(jax.random.fold_in(stream_key, 6), dim), (blocks,), jnp.float32, low / len(cuts), high / len(cuts))
        return jnp.repeat(jnp.exp(heights), shape[dim] // blocks).reshape((-1,) + (1,) * (len(shape) - dim - 1))

    loudness = one(*cuts[0])
    for cut in cuts[1:]:
        loudness = loudness * one(*cut)
    return loudness


def gaussian(own_key, dims, scale, reach, cuts=(), kind=jnp.bfloat16):
    drawn = scale * jax.random.normal(own_key, dims, jnp.float32)
    if cuts:
        drawn = drawn * block_scale(own_key, dims, cuts, -0.22, 0.18)
    return jnp.clip(drawn, -reach, reach).astype(kind)


def setup_inputs(seed: int = 0) -> dict:
    key_list = jax.random.split(jax.random.key(seed), 4)
    return {
        "coadd_flux": gaussian(key_list[0], (NR, NC), 1.0, 8.0, ((0, 32), (1, 16)), jnp.float32),
        "inverse_variance": jnp.clip(jnp.exp(math.log(4.0) - 2.7725887 * jax.random.uniform(key_list[1], (NR, NC), jnp.float32) ** block_scale(key_list[1], (NR, NC), ((0, 32), (1, 16)), -0.2, 0.2)), 0.25, 4.0),
        "source_mask": with_ends((jax.random.randint(key_list[2], (NR, NC), 0, 4) < 1).astype(jnp.int32), jax.random.fold_in(key_list[2], 1), 0, 1),
    }


smooth_weight = 2.0
blur_sigma = 10.0

def apply_operator(field, weight):
    padded = jnp.pad(field, 1)
    beside = padded[2:, 1:-1] + padded[:-2, 1:-1] + padded[1:-1, 2:] + padded[1:-1, :-2]
    return weight * field + smooth_weight * (4.0 * field - beside)

def tap_values():
    offsets = jnp.arange(2 * RADIUS + 1).astype(jnp.float32) - RADIUS
    raw_taps = jnp.exp(-offsets * offsets / (2.0 * blur_sigma * blur_sigma))
    return raw_taps / jnp.sum(raw_taps)

def blur_leading(field):
    taps = tap_values()
    padded = jnp.pad(field, ((RADIUS, RADIUS), (0, 0)))
    length = field.shape[0]
    summed = jnp.zeros_like(field)
    for offset in range(2 * RADIUS + 1):
        summed = summed + taps[offset] * padded[offset:offset + length]
    return summed

def reference(coadd_flux, inverse_variance, source_mask):
    weight = inverse_variance * (1.0 - source_mask.astype(jnp.float32))
    background = jnp.zeros_like(coadd_flux)
    residual = weight * coadd_flux
    direction = residual
    norm_now = jnp.sum(residual * residual)
    for step in range(ITERS):
        image_term = apply_operator(direction, weight)
        alpha = norm_now / jnp.sum(direction * image_term)
        background = background + alpha * direction
        residual = residual - alpha * image_term
        if step + 1 < ITERS:
            norm_next = jnp.sum(residual * residual)
            direction = residual + norm_next / norm_now * direction
            norm_now = norm_next
    scatter = coadd_flux - background
    smoothed = scatter * scatter
    for repeat in range(2):
        smoothed = blur_leading(smoothed)
        smoothed = blur_leading(smoothed.T).T
    return (background, jnp.sqrt(smoothed + 1e-06))
```

```python
import functools

import jax
import jax.numpy as jnp
import numpy as np
from jax import lax
from jax.experimental import pallas as pl
from jax.experimental.pallas import tpu as pltpu
from jax.sharding import PartitionSpec as P

RADIUS = 32
SIGMA = 10.0
SMOOTH = 2.0
REACH = 2 * RADIUS
ROWS, COLS = 32, 16
H, W = 128, 1024
HB = 72
LANE = 128
EW = W + 2 * LANE
BH = H + 2 * HB
SH, SW = H + 2 * REACH, W + 2 * REACH
PH = H + 24
MESH = pl.DeviceIdType.MESH
TAP_SUM = float(np.sum(np.exp(-np.arange(-RADIUS, RADIUS + 1) ** 2 / (2.0 * SIGMA * SIGMA))))
F32 = jnp.float32
BF16 = jnp.bfloat16


def tap(distance):
    d = distance.astype(F32)
    value = jnp.exp(-d * d / (2.0 * SIGMA * SIGMA)) / TAP_SUM
    return jnp.where(jnp.abs(distance) <= RADIUS, value, 0.0)


def iota(shape, dim):
    return lax.broadcasted_iota(jnp.int32, shape, dim)


def split(x):
    high = x.astype(BF16)
    return high, (x - high.astype(F32)).astype(BF16)


def dot32(a, b):
    return jnp.dot(a, b, precision=lax.Precision.HIGHEST, preferred_element_type=F32)


def total(x):
    return jnp.sum(jnp.sum(x, axis=0, keepdims=True), axis=1, keepdims=True)


def gather_kernel(
    f_hbm, iv_hbm, mk_hbm,
    fx, ux, vx, uc, vc, row_taps, col_taps, sums,
    fb, wb, ub, ivb, mkb, up, wp, vp, col_out, col_in, msg, slots_p, slots_z,
    load_sem, near_send, near_recv, wide_send, wide_recv, p_send, p_recv, z_send, z_recv,
):
    r, z = lax.axis_index("rows"), lax.axis_index("cols")
    r_up, r_dn = lax.rem(r + ROWS - 1, ROWS), lax.rem(r + 1, ROWS)
    z_lf, z_rt = lax.rem(z + COLS - 1, COLS), lax.rem(z + 1, COLS)
    has_up, has_dn, has_lf, has_rt = r > 0, r < ROWS - 1, z > 0, z < COLS - 1

    loads = [
        pltpu.make_async_copy(f_hbm, fb.at[pl.ds(HB, H), pl.ds(LANE, W)], load_sem.at[0]),
        pltpu.make_async_copy(iv_hbm, ivb, load_sem.at[1]),
        pltpu.make_async_copy(mk_hbm, mkb, load_sem.at[2]),
    ]
    for c in loads:
        c.start()
    up[0:8, :] = jnp.zeros((8, EW), F32)
    up[H + 8 : PH, :] = jnp.zeros((16, EW), F32)
    wp[H + 8 : PH, :] = jnp.zeros((16, EW), F32)

    barrier = pltpu.get_barrier_semaphore()
    count = 0
    for k in range(1, ROWS):
        pl.semaphore_signal(barrier, inc=1, device_id=(lax.rem(r + k, ROWS), z), device_id_type=MESH)
        count += 1
    for k in range(1, COLS):
        pl.semaphore_signal(barrier, inc=1, device_id=(r, lax.rem(z + k, COLS)), device_id_type=MESH)
        count += 1
    for a in (r_up, r_dn):
        for b in (z_lf, z_rt):
            pl.semaphore_signal(barrier, inc=1, device_id=(a, b), device_id_type=MESH)
            count += 1

    for c in loads:
        c.wait()

    def weigh(s, _):
        rows = pl.ds(pl.multiple_of(s * 8, 8), 8)
        w = ivb[rows, :] * (1.0 - mkb[rows, :].astype(F32))
        wb[pl.ds(pl.multiple_of(s * 8 + HB, 8), 8), LANE : LANE + W] = w
        here = pl.ds(pl.multiple_of(s * 8 + 8, 8), 8)
        wp[here, LANE : LANE + W] = w
        u = w * fb[pl.ds(pl.multiple_of(s * 8 + HB, 8), 8), LANE : LANE + W]
        up[here, LANE : LANE + W] = u
        uc[rows, :] = u
        return 0

    lax.fori_loop(0, H // 8, weigh, 0)
    left_cols = jnp.transpose(up[8 : H + 8, LANE : 2 * LANE])
    col_out[0] = left_cols[0:8, :]
    col_out[1] = jnp.transpose(wp[8 : H + 8, LANE : 2 * LANE])[0:8, :]
    col_out[2] = jnp.transpose(up[8 : H + 8, W : W + LANE])[LANE - 8 : LANE, :]

    pl.semaphore_wait(barrier, count)

    near = []

    def near_copy(src, dst, device, send_if, recv_if):
        k = len(near)
        c = pltpu.make_async_remote_copy(
            src_ref=src, dst_ref=dst, send_sem=near_send.at[k], recv_sem=near_recv.at[k],
            device_id=device, device_id_type=MESH,
        )
        near.append((c, send_if, recv_if))

    first, last = pl.ds(8, 8), pl.ds(H, 8)
    top, below = pl.ds(0, 8), pl.ds(H + 8, 8)
    mid, lf, rt = pl.ds(LANE, W), pl.ds(0, LANE), pl.ds(LANE + W, LANE)
    c_first, c_last = pl.ds(LANE, LANE), pl.ds(W, LANE)
    near_copy(up.at[first, mid], up.at[below, mid], (r_up, z), has_up, has_dn)
    near_copy(wp.at[first, mid], wp.at[below, mid], (r_up, z), has_up, has_dn)
    near_copy(up.at[last, mid], up.at[top, mid], (r_dn, z), has_dn, has_up)
    near_copy(col_out.at[0], col_in.at[0], (r, z_lf), has_lf, has_rt)
    near_copy(col_out.at[1], col_in.at[1], (r, z_lf), has_lf, has_rt)
    near_copy(col_out.at[2], col_in.at[2], (r, z_rt), has_rt, has_lf)
    near_copy(up.at[last, c_first], up.at[top, rt], (r_dn, z_lf), has_dn & has_lf, has_up & has_rt)
    near_copy(up.at[first, c_first], up.at[below, rt], (r_up, z_lf), has_up & has_lf, has_dn & has_rt)
    near_copy(up.at[first, c_last], up.at[below, lf], (r_up, z_rt), has_up & has_rt, has_dn & has_lf)
    for c, send_if, _ in near:
        pl.when(send_if)(c.start)
    for c, _, recv_if in near:
        pl.when(recv_if)(c.wait_recv)

    pad = jnp.zeros((LANE - 8, LANE), F32)

    def column(x, there):
        return jnp.where(there, x, jnp.zeros_like(x))

    up[8 : H + 8, LANE + W : EW] = jnp.transpose(jnp.concatenate([column(col_in[0], has_rt), pad], axis=0))
    wp[8 : H + 8, LANE + W : EW] = jnp.transpose(jnp.concatenate([column(col_in[1], has_rt), pad], axis=0))
    up[8 : H + 8, 0:LANE] = jnp.transpose(jnp.concatenate([pad, column(col_in[2], has_lf)], axis=0))

    cols8 = iota((8, EW), 1) - LANE
    rows8 = iota((8, EW), 0)

    def higher(src, row, x):
        before = src[pl.ds(pl.multiple_of(row - 8, 8), 8), :]
        return pltpu.roll(jnp.where(rows8 == 7, before, x), 1, 0)

    def lower(src, row, x):
        after = src[pl.ds(pl.multiple_of(row + 8, 8), 8), :]
        return pltpu.roll(jnp.where(rows8 == 0, after, x), 7, 0)

    def operator(src, row, u, w):
        above, under = higher(src, row, u), lower(src, row, u)
        beside = above + under + pltpu.roll(u, 1, 1) + pltpu.roll(u, EW - 1, 1)
        return w * u + SMOOTH * (4.0 * u - beside)

    def image(s, _):
        row = pl.multiple_of(s * 8 + 8, 8)
        here = pl.ds(row, 8)
        v = operator(up, row, up[here, :], wp[here, :])
        inside = ((rows8 + s * 8 < H) | has_dn) & ((cols8 < W) | has_rt)
        vp[here, :] = jnp.where(inside, v, 0.0)
        return 0

    lax.fori_loop(0, H // 8 + 1, image, 0)

    def add_up(s, acc):
        row = pl.multiple_of(s * 8 + 8, 8)
        here = pl.ds(row, 8)
        u, w, v = up[here, :], wp[here, :], vp[here, :]
        dn = v - lower(vp, row, v)
        rt_ = v - pltpu.roll(v, EW - 1, 1)
        edge = ((s == 0) & (r == 0) & (rows8 == 0)).astype(F32) + ((cols8 == 0) & (z == 0)).astype(F32)
        vv = v * v
        terms = (u * u, u * v, vv, w * vv + SMOOTH * (dn * dn + rt_ * rt_ + edge * vv))
        vc[pl.ds(pl.multiple_of(s * 8, 8), 8), :] = v[:, LANE : LANE + W]
        return tuple(a + t[:, LANE : LANE + W] for a, t in zip(acc, terms))

    acc = lax.fori_loop(0, H // 8, add_up, tuple(jnp.zeros((8, W), F32) for _ in range(4)))
    lane = iota((1, LANE), 1)
    packed = jnp.zeros((1, LANE), F32)
    for k, a in enumerate(acc):
        packed = jnp.where(lane == k, total(a), packed)
    msg[0] = packed

    def exchange(mine, slots, me, number, device, send_sem, recv_sem):
        copies = [
            pltpu.make_async_remote_copy(
                src_ref=mine, dst_ref=slots.at[me], send_sem=send_sem, recv_sem=recv_sem,
                device_id=device(lax.rem(me + k, number)), device_id_type=MESH,
            )
            for k in range(1, number)
        ]
        for c in copies:
            c.start()
        slots[me] = mine[...]

    def settle(slots, number, sems):
        arrivals = slots.at[pl.ds(0, number - 1)]
        for sem in sems:
            pltpu.make_async_copy(arrivals, arrivals, sem).wait()

    exchange(msg.at[0], slots_p, r, ROWS, lambda i: (i, z), p_send, p_recv)

    wide = []

    def wide_copy(src_rows, src_cols, dst_rows, dst_cols, device, send_if, recv_if):
        for buf in (fb, wb):
            k = len(wide)
            c = pltpu.make_async_remote_copy(
                src_ref=buf.at[src_rows, src_cols], dst_ref=buf.at[dst_rows, dst_cols],
                send_sem=wide_send.at[k], recv_sem=wide_recv.at[k], device_id=device, device_id_type=MESH,
            )
            wide.append((c, send_if, recv_if))

    first, last, every = pl.ds(HB, HB), pl.ds(H, HB), pl.ds(HB, H)
    top, below = pl.ds(0, HB), pl.ds(HB + H, HB)
    wide_copy(every, c_first, every, rt, (r, z_lf), has_lf, has_rt)
    wide_copy(every, c_last, every, lf, (r, z_rt), has_rt, has_lf)
    wide_copy(first, mid, below, mid, (r_up, z), has_up, has_dn)
    wide_copy(last, mid, top, mid, (r_dn, z), has_dn, has_up)
    wide_copy(first, c_first, below, rt, (r_up, z_lf), has_up & has_lf, has_dn & has_rt)
    wide_copy(first, c_last, below, lf, (r_up, z_rt), has_up & has_rt, has_dn & has_lf)
    wide_copy(last, c_first, top, rt, (r_dn, z_lf), has_dn & has_lf, has_up & has_rt)
    wide_copy(last, c_last, top, lf, (r_dn, z_rt), has_dn & has_rt, has_up & has_lf)
    for c, send_if, _ in wide:
        pl.when(send_if)(c.start)

    settle(slots_p, ROWS, (p_send, p_recv))
    msg[1] = jnp.sum(slots_p[...], axis=0)
    exchange(msg.at[1], slots_z, z, COLS, lambda i: (r, i), z_send, z_recv)

    def square(height, width):
        return iota((height, width), 0), iota((height, width), 1)

    i, k = square(H, 256)
    at = r * H - REACH + k
    one = jnp.where((at >= 0) & (at < ROWS * H), tap(k - REACH - i), 0.0)
    k, j = square(256, 256)
    high, low = split(dot32(one, tap(k - j)))
    row_taps[0:H, :] = high
    row_taps[H : 2 * H, :] = low
    for n, t in enumerate((0, 3, 7)):
        j, k = square(256, 256)
        at = z * W + t * LANE - REACH + k
        one = jnp.where((at >= 0) & (at < COLS * W), tap(j - k), 0.0)
        k, i = square(256, LANE)
        high, low = split(dot32(one, tap(k - REACH - i)))
        col_taps[n, :, 0:LANE] = high
        col_taps[n, :, LANE : 2 * LANE] = low

    for c, _, recv_if in wide:
        pl.when(recv_if)(c.wait_recv)

    def inside(row):
        at_row, at_col = rows8 + row + (r * H - HB), cols8 + z * W
        return (at_row >= 0) & (at_row < ROWS * H) & (at_col >= 0) & (at_col < COLS * W)

    def weighted(s, _):
        row = pl.multiple_of(s * 8, 8)
        here = pl.ds(row, 8)
        ub[here, :] = jnp.where(inside(row), fb[here, :] * wb[here, :], 0.0)
        return 0

    lax.fori_loop(0, BH // 8, weighted, 0)

    def extend(s, _):
        row = pl.multiple_of(s * 8 + 8, 8)
        here, there = pl.ds(row, 8), pl.ds(pl.multiple_of(s * 8, 8), 8)
        keep = inside(row)
        u = ub[here, :]
        v = jnp.where(keep, operator(ub, row, u, wb[here, :]), 0.0)
        f = jnp.where(keep, fb[here, :], 0.0)
        for dst, x in ((fx, f), (ux, u), (vx, v)):
            dst[there, :] = pltpu.roll(x, EW - (LANE - REACH), 1)[:, 0:SW]
        return 0

    lax.fori_loop(0, SH // 8, extend, 0)

    settle(slots_z, COLS, (z_send, z_recv))
    sums[...] = jnp.sum(slots_z[...], axis=0)

    for c, send_if, _ in near + wide:
        pl.when(send_if)(c.wait_send)


def blur_kernel(fx, ux, vx, uc, vc, row_taps, col_taps, sums, background, rms):
    g = sums[...]
    uu, uau, vv, vav = (g[0:1, k : k + 1] for k in range(4))
    alpha = uu / uau
    new = alpha * alpha * vv - uu
    keep = 1.0 + new / uu
    curve = keep * keep * uau - 2.0 * keep * alpha * vv + alpha * alpha * vav
    alpha1 = new / curve
    on_u = alpha + alpha1 * keep
    on_v = alpha1 * alpha
    background[...] = on_u * uc[...] - on_v * vc[...]
    taps_hl, taps_h = row_taps[...], row_taps[0:H, :]
    wide = SW // 2
    parts = []
    for start in (0, wide // LANE * LANE, SW):
        parts.append(start)
    highs, lows = [], []
    for a, b in zip(parts[:-1], parts[1:]):
        s = fx[:, a:b] - (on_u * ux[:, a:b] - on_v * vx[:, a:b])
        high, low = split(s * s)
        both = jnp.dot(taps_hl, high, preferred_element_type=F32)
        y = both[0:H] + both[H : 2 * H] + jnp.dot(taps_h, low, preferred_element_type=F32)
        high, low = split(y)
        highs.append(high)
        lows.append(low)
    yh, yl = jnp.concatenate(highs, axis=1), jnp.concatenate(lows, axis=1)
    for t in range(W // LANE):
        n = 0 if t == 0 else 2 if t == W // LANE - 1 else 1
        window = slice(t * LANE, t * LANE + 256)
        both = jnp.dot(yh[:, window], col_taps[n], preferred_element_type=F32)
        out = both[:, 0:LANE] + both[:, LANE:]
        out = out + jnp.dot(yl[:, window], col_taps[n, :, 0:LANE], preferred_element_type=F32)
        rms[:, t * LANE : (t + 1) * LANE] = jnp.sqrt(out + 1e-06)


def block(coadd_flux, inverse_variance, source_mask):
    vmem = pl.BlockSpec(memory_space=pltpu.VMEM)
    anywhere = pl.BlockSpec(memory_space=pl.ANY)
    fields = [jax.ShapeDtypeStruct((SH, SW), F32)] * 3 + [jax.ShapeDtypeStruct((H, W), F32)] * 2
    fields += [jax.ShapeDtypeStruct((2 * H, 256), BF16), jax.ShapeDtypeStruct((3, 256, 256), BF16)]
    fields += [jax.ShapeDtypeStruct((1, LANE), F32)]
    dma = pltpu.SemaphoreType.DMA
    mids = pl.pallas_call(
        gather_kernel,
        out_shape=fields,
        in_specs=[anywhere] * 3,
        out_specs=[vmem] * len(fields),
        scratch_shapes=[
            pltpu.VMEM((BH, EW), F32), pltpu.VMEM((BH, EW), F32), pltpu.VMEM((BH, EW), F32),
            pltpu.VMEM((H, W), F32), pltpu.VMEM((H, W), jnp.int32),
            pltpu.VMEM((PH, EW), F32), pltpu.VMEM((PH, EW), F32), pltpu.VMEM((PH, EW), F32),
            pltpu.VMEM((3, 8, LANE), F32), pltpu.VMEM((3, 8, LANE), F32),
            pltpu.VMEM((2, 1, LANE), F32), pltpu.VMEM((ROWS, 1, LANE), F32), pltpu.VMEM((COLS, 1, LANE), F32),
            dma((3,)), dma((9,)), dma((9,)), dma((16,)), dma((16,)), dma, dma, dma, dma,
        ],
        compiler_params=pltpu.CompilerParams(collective_id=0, has_side_effects=True),
        name="gather",
    )(coadd_flux, inverse_variance, source_mask)
    return pl.pallas_call(
        blur_kernel,
        out_shape=[jax.ShapeDtypeStruct((H, W), F32)] * 2,
        in_specs=[vmem] * len(fields),
        out_specs=[vmem] * 2,
        name="blur",
    )(*mids)


def solution(mesh):
    return jax.shard_map(
        block,
        mesh=mesh,
        in_specs=(P("rows", "cols"),) * 3,
        out_specs=(P("rows", "cols"),) * 2,
        check_vma=False,
    )
```

```python
import functools

import jax
import jax.numpy as jnp
import numpy as np
from jax import lax
from jax.experimental import pallas as pl
from jax.experimental.pallas import tpu as pltpu
from jax.sharding import PartitionSpec as P

RADIUS = 32
SIGMA = 10.0
SMOOTH = 2.0
REACH = 2 * RADIUS
ROWS, COLS = 32, 16
H, W = 128, 1024
HB = 72
LANE = 128
EW = W + 2 * LANE
BH = H + 2 * HB
SH, SW = H + 2 * REACH, W + 2 * REACH
PH = H + 24
MESH = pl.DeviceIdType.MESH
TAP_SUM = float(np.sum(np.exp(-np.arange(-RADIUS, RADIUS + 1) ** 2 / (2.0 * SIGMA * SIGMA))))
F32 = jnp.float32
BF16 = jnp.bfloat16


def tap(distance):
    d = distance.astype(F32)
    value = jnp.exp(-d * d / (2.0 * SIGMA * SIGMA)) / TAP_SUM
    return jnp.where(jnp.abs(distance) <= RADIUS, value, 0.0)


def iota(shape, dim):
    return lax.broadcasted_iota(jnp.int32, shape, dim)


def split(x):
    high = x.astype(BF16)
    return high, (x - high.astype(F32)).astype(BF16)


def dot32(a, b):
    return jnp.dot(a, b, precision=lax.Precision.HIGHEST, preferred_element_type=F32)


def total(x):
    return jnp.sum(jnp.sum(x, axis=0, keepdims=True), axis=1, keepdims=True)


def gather_kernel(
    f_hbm, iv_hbm, mk_hbm,
    fx, ux, vx, uc, vc, row_taps, col_taps, sums,
    fb, wb, ub, ivb, mkb, up, wp, vp, col_out, col_in, msg, slots_p, slots_z,
    load_sem, near_send, near_recv, wide_send, wide_recv, p_send, p_recv, z_send, z_recv, chain,
):
    r, z = lax.axis_index("rows"), lax.axis_index("cols")
    r_up, r_dn = lax.rem(r + ROWS - 1, ROWS), lax.rem(r + 1, ROWS)
    z_lf, z_rt = lax.rem(z + COLS - 1, COLS), lax.rem(z + 1, COLS)
    has_up, has_dn, has_lf, has_rt = r > 0, r < ROWS - 1, z > 0, z < COLS - 1

    loads = [
        pltpu.make_async_copy(f_hbm, fb.at[pl.ds(HB, H), pl.ds(LANE, W)], load_sem.at[0]),
        pltpu.make_async_copy(iv_hbm, ivb, load_sem.at[1]),
        pltpu.make_async_copy(mk_hbm, mkb, load_sem.at[2]),
    ]
    for c in loads:
        c.start()
    up[0:8, :] = jnp.zeros((8, EW), F32)
    up[H + 8 : PH, :] = jnp.zeros((16, EW), F32)
    wp[H + 8 : PH, :] = jnp.zeros((16, EW), F32)

    barrier = pltpu.get_barrier_semaphore()
    count = 0
    for k in range(1, ROWS):
        pl.semaphore_signal(barrier, inc=1, device_id=(lax.rem(r + k, ROWS), z), device_id_type=MESH)
        count += 1
    for b in (z_lf, z_rt):
        pl.semaphore_signal(barrier, inc=1, device_id=(r, b), device_id_type=MESH)
        count += 1
    for a in (r_up, r_dn):
        for b in (z_lf, z_rt):
            pl.semaphore_signal(barrier, inc=1, device_id=(a, b), device_id_type=MESH)
            count += 1

    for c in loads:
        c.wait()

    def weigh(s, _):
        rows = pl.ds(pl.multiple_of(s * 8, 8), 8)
        w = ivb[rows, :] * (1.0 - mkb[rows, :].astype(F32))
        wb[pl.ds(pl.multiple_of(s * 8 + HB, 8), 8), LANE : LANE + W] = w
        here = pl.ds(pl.multiple_of(s * 8 + 8, 8), 8)
        wp[here, LANE : LANE + W] = w
        u = w * fb[pl.ds(pl.multiple_of(s * 8 + HB, 8), 8), LANE : LANE + W]
        up[here, LANE : LANE + W] = u
        uc[rows, :] = u
        return 0

    lax.fori_loop(0, H // 8, weigh, 0)
    left_cols = jnp.transpose(up[8 : H + 8, LANE : 2 * LANE])
    col_out[0] = left_cols[0:8, :]
    col_out[1] = jnp.transpose(wp[8 : H + 8, LANE : 2 * LANE])[0:8, :]
    col_out[2] = jnp.transpose(up[8 : H + 8, W : W + LANE])[LANE - 8 : LANE, :]

    pl.semaphore_wait(barrier, count)

    def entered(step):
        for away in (1 << step, COLS - (1 << step)):
            pl.semaphore_signal(chain.at[step], inc=1, device_id=(r, lax.rem(z + away, COLS)), device_id_type=MESH)

    entered(0)

    near = []

    def near_copy(src, dst, device, send_if, recv_if):
        k = len(near)
        c = pltpu.make_async_remote_copy(
            src_ref=src, dst_ref=dst, send_sem=near_send.at[k], recv_sem=near_recv.at[k],
            device_id=device, device_id_type=MESH,
        )
        near.append((c, send_if, recv_if))

    first, last = pl.ds(8, 8), pl.ds(H, 8)
    top, below = pl.ds(0, 8), pl.ds(H + 8, 8)
    mid, lf, rt = pl.ds(LANE, W), pl.ds(0, LANE), pl.ds(LANE + W, LANE)
    c_first, c_last = pl.ds(LANE, LANE), pl.ds(W, LANE)
    near_copy(up.at[first, mid], up.at[below, mid], (r_up, z), has_up, has_dn)
    near_copy(wp.at[first, mid], wp.at[below, mid], (r_up, z), has_up, has_dn)
    near_copy(up.at[last, mid], up.at[top, mid], (r_dn, z), has_dn, has_up)
    near_copy(col_out.at[0], col_in.at[0], (r, z_lf), has_lf, has_rt)
    near_copy(col_out.at[1], col_in.at[1], (r, z_lf), has_lf, has_rt)
    near_copy(col_out.at[2], col_in.at[2], (r, z_rt), has_rt, has_lf)
    near_copy(up.at[last, c_first], up.at[top, rt], (r_dn, z_lf), has_dn & has_lf, has_up & has_rt)
    near_copy(up.at[first, c_first], up.at[below, rt], (r_up, z_lf), has_up & has_lf, has_dn & has_rt)
    near_copy(up.at[first, c_last], up.at[below, lf], (r_up, z_rt), has_up & has_rt, has_dn & has_lf)
    for c, send_if, _ in near:
        pl.when(send_if)(c.start)
    wide = []

    def wide_copy(src_rows, src_cols, dst_rows, dst_cols, device, send_if, recv_if):
        for buf in (fb, wb):
            k = len(wide)
            c = pltpu.make_async_remote_copy(
                src_ref=buf.at[src_rows, src_cols], dst_ref=buf.at[dst_rows, dst_cols],
                send_sem=wide_send.at[k], recv_sem=wide_recv.at[k], device_id=device, device_id_type=MESH,
            )
            wide.append((c, send_if, recv_if))

    w_first, w_last, every = pl.ds(HB, HB), pl.ds(H, HB), pl.ds(HB, H)
    w_top, w_below = pl.ds(0, HB), pl.ds(HB + H, HB)
    wide_copy(every, c_first, every, rt, (r, z_lf), has_lf, has_rt)
    wide_copy(every, c_last, every, lf, (r, z_rt), has_rt, has_lf)
    wide_copy(w_first, mid, w_below, mid, (r_up, z), has_up, has_dn)
    wide_copy(w_last, mid, w_top, mid, (r_dn, z), has_dn, has_up)
    wide_copy(w_first, c_first, w_below, rt, (r_up, z_lf), has_up & has_lf, has_dn & has_rt)
    wide_copy(w_first, c_last, w_below, lf, (r_up, z_rt), has_up & has_rt, has_dn & has_lf)
    wide_copy(w_last, c_first, w_top, rt, (r_dn, z_lf), has_dn & has_lf, has_up & has_rt)
    wide_copy(w_last, c_last, w_top, lf, (r_dn, z_rt), has_dn & has_rt, has_up & has_lf)
    early = [n for n in range(len(wide)) if n not in (5, 7)]
    late = [5, 7]
    for n in early:
        pl.when(wide[n][1])(wide[n][0].start)

    pl.semaphore_wait(chain.at[0], 2)
    entered(1)
    for c, _, recv_if in near:
        pl.when(recv_if)(c.wait_recv)

    pad = jnp.zeros((LANE - 8, LANE), F32)

    def column(x, there):
        return jnp.where(there, x, jnp.zeros_like(x))

    up[8 : H + 8, LANE + W : EW] = jnp.transpose(jnp.concatenate([column(col_in[0], has_rt), pad], axis=0))
    wp[8 : H + 8, LANE + W : EW] = jnp.transpose(jnp.concatenate([column(col_in[1], has_rt), pad], axis=0))
    up[8 : H + 8, 0:LANE] = jnp.transpose(jnp.concatenate([pad, column(col_in[2], has_lf)], axis=0))

    cols8 = iota((8, EW), 1) - LANE
    rows8 = iota((8, EW), 0)

    def higher(src, row, x):
        before = src[pl.ds(pl.multiple_of(row - 8, 8), 8), :]
        return pltpu.roll(jnp.where(rows8 == 7, before, x), 1, 0)

    def lower(src, row, x):
        after = src[pl.ds(pl.multiple_of(row + 8, 8), 8), :]
        return pltpu.roll(jnp.where(rows8 == 0, after, x), 7, 0)

    def operator(src, row, u, w):
        above, under = higher(src, row, u), lower(src, row, u)
        beside = above + under + pltpu.roll(u, 1, 1) + pltpu.roll(u, EW - 1, 1)
        return w * u + SMOOTH * (4.0 * u - beside)

    def image(s, _):
        row = pl.multiple_of(s * 8 + 8, 8)
        here = pl.ds(row, 8)
        v = operator(up, row, up[here, :], wp[here, :])
        inside = ((rows8 + s * 8 < H) | has_dn) & ((cols8 < W) | has_rt)
        vp[here, :] = jnp.where(inside, v, 0.0)
        return 0

    lax.fori_loop(0, H // 8 + 1, image, 0)

    def add_up(s, acc):
        row = pl.multiple_of(s * 8 + 8, 8)
        here = pl.ds(row, 8)
        u, w, v = up[here, :], wp[here, :], vp[here, :]
        dn = v - lower(vp, row, v)
        rt_ = v - pltpu.roll(v, EW - 1, 1)
        edge = ((s == 0) & (r == 0) & (rows8 == 0)).astype(F32) + ((cols8 == 0) & (z == 0)).astype(F32)
        vv = v * v
        terms = (u * u, u * v, vv, w * vv + SMOOTH * (dn * dn + rt_ * rt_ + edge * vv))
        vc[pl.ds(pl.multiple_of(s * 8, 8), 8), :] = v[:, LANE : LANE + W]
        return tuple(a + t[:, LANE : LANE + W] for a, t in zip(acc, terms))

    acc = lax.fori_loop(0, H // 8, add_up, tuple(jnp.zeros((8, W), F32) for _ in range(4)))
    lane = iota((1, LANE), 1)
    packed = jnp.zeros((1, LANE), F32)
    for k, a in enumerate(acc):
        packed = jnp.where(lane == k, total(a), packed)
    msg[0] = packed

    def exchange(mine, slots, me, number, device, send_sem, recv_sem):
        copies = [
            pltpu.make_async_remote_copy(
                src_ref=mine, dst_ref=slots.at[me], send_sem=send_sem, recv_sem=recv_sem,
                device_id=device(lax.rem(me + k, number)), device_id_type=MESH,
            )
            for k in range(1, number)
        ]
        for c in copies:
            c.start()
        slots[me] = mine[...]

    def settle(slots, number, sems):
        arrivals = slots.at[pl.ds(0, number - 1)]
        for sem in sems:
            pltpu.make_async_copy(arrivals, arrivals, sem).wait()

    exchange(msg.at[0], slots_p, r, ROWS, lambda i: (i, z), p_send, p_recv)

    for n in late:
        pl.when(wide[n][1])(wide[n][0].start)
    pl.semaphore_wait(chain.at[1], 2)
    entered(2)
    def square(height, width):
        return iota((height, width), 0), iota((height, width), 1)

    i, k = square(H, 256)
    at = r * H - REACH + k
    one = jnp.where((at >= 0) & (at < ROWS * H), tap(k - REACH - i), 0.0)
    k, j = square(256, 256)
    high, low = split(dot32(one, tap(k - j)))
    row_taps[0:H, :] = high
    row_taps[H : 2 * H, :] = low
    for n, t in enumerate((0, 3, 7)):
        j, k = square(256, 256)
        at = z * W + t * LANE - REACH + k
        one = jnp.where((at >= 0) & (at < COLS * W), tap(j - k), 0.0)
        k, i = square(256, LANE)
        high, low = split(dot32(one, tap(k - REACH - i)))
        col_taps[n, :, 0:LANE] = high
        col_taps[n, :, LANE : 2 * LANE] = low

    settle(slots_p, ROWS, (p_send, p_recv))
    msg[1] = jnp.sum(slots_p[...], axis=0)
    pl.semaphore_wait(chain.at[2], 2)
    exchange(msg.at[1], slots_z, z, COLS, lambda i: (r, i), z_send, z_recv)

    for c, _, recv_if in wide:
        pl.when(recv_if)(c.wait_recv)

    def inside(row):
        at_row, at_col = rows8 + row + (r * H - HB), cols8 + z * W
        return (at_row >= 0) & (at_row < ROWS * H) & (at_col >= 0) & (at_col < COLS * W)

    def weighted(s, _):
        row = pl.multiple_of(s * 8, 8)
        here = pl.ds(row, 8)
        ub[here, :] = jnp.where(inside(row), fb[here, :] * wb[here, :], 0.0)
        return 0

    lax.fori_loop(0, BH // 8, weighted, 0)

    def extend(s, _):
        row = pl.multiple_of(s * 8 + 8, 8)
        here, there = pl.ds(row, 8), pl.ds(pl.multiple_of(s * 8, 8), 8)
        keep = inside(row)
        u = ub[here, :]
        v = jnp.where(keep, operator(ub, row, u, wb[here, :]), 0.0)
        f = jnp.where(keep, fb[here, :], 0.0)
        for dst, x in ((fx, f), (ux, u), (vx, v)):
            dst[there, :] = pltpu.roll(x, EW - (LANE - REACH), 1)[:, 0:SW]
        return 0

    lax.fori_loop(0, SH // 8, extend, 0)

    settle(slots_z, COLS, (z_send, z_recv))
    sums[...] = jnp.sum(slots_z[...], axis=0)

    for c, send_if, _ in near + wide:
        pl.when(send_if)(c.wait_send)


def blur_kernel(fx, ux, vx, uc, vc, row_taps, col_taps, sums, background, rms):
    g = sums[...]
    uu, uau, vv, vav = (g[0:1, k : k + 1] for k in range(4))
    alpha = uu / uau
    new = alpha * alpha * vv - uu
    keep = 1.0 + new / uu
    curve = keep * keep * uau - 2.0 * keep * alpha * vv + alpha * alpha * vav
    alpha1 = new / curve
    on_u = alpha + alpha1 * keep
    on_v = alpha1 * alpha
    background[...] = on_u * uc[...] - on_v * vc[...]
    taps_hl, taps_h = row_taps[...], row_taps[0:H, :]
    wide = SW // 2
    parts = []
    for start in (0, wide // LANE * LANE, SW):
        parts.append(start)
    highs, lows = [], []
    for a, b in zip(parts[:-1], parts[1:]):
        s = fx[:, a:b] - (on_u * ux[:, a:b] - on_v * vx[:, a:b])
        high, low = split(s * s)
        both = jnp.dot(taps_hl, high, preferred_element_type=F32)
        y = both[0:H] + both[H : 2 * H] + jnp.dot(taps_h, low, preferred_element_type=F32)
        high, low = split(y)
        highs.append(high)
        lows.append(low)
    yh, yl = jnp.concatenate(highs, axis=1), jnp.concatenate(lows, axis=1)
    for t in range(W // LANE):
        n = 0 if t == 0 else 2 if t == W // LANE - 1 else 1
        window = slice(t * LANE, t * LANE + 256)
        both = jnp.dot(yh[:, window], col_taps[n], preferred_element_type=F32)
        out = both[:, 0:LANE] + both[:, LANE:]
        out = out + jnp.dot(yl[:, window], col_taps[n, :, 0:LANE], preferred_element_type=F32)
        rms[:, t * LANE : (t + 1) * LANE] = jnp.sqrt(out + 1e-06)


def block(coadd_flux, inverse_variance, source_mask):
    vmem = pl.BlockSpec(memory_space=pltpu.VMEM)
    anywhere = pl.BlockSpec(memory_space=pltpu.HBM)
    fields = [jax.ShapeDtypeStruct((SH, SW), F32)] * 3 + [jax.ShapeDtypeStruct((H, W), F32)] * 2
    fields += [jax.ShapeDtypeStruct((2 * H, 256), BF16), jax.ShapeDtypeStruct((3, 256, 256), BF16)]
    fields += [jax.ShapeDtypeStruct((1, LANE), F32)]
    dma = pltpu.SemaphoreType.DMA
    mids = pl.pallas_call(
        gather_kernel,
        out_shape=fields,
        in_specs=[anywhere] * 3,
        out_specs=[vmem] * len(fields),
        scratch_shapes=[
            pltpu.VMEM((BH, EW), F32), pltpu.VMEM((BH, EW), F32), pltpu.VMEM((BH, EW), F32),
            pltpu.VMEM((H, W), F32), pltpu.VMEM((H, W), jnp.int32),
            pltpu.VMEM((PH, EW), F32), pltpu.VMEM((PH, EW), F32), pltpu.VMEM((PH, EW), F32),
            pltpu.VMEM((3, 8, LANE), F32), pltpu.VMEM((3, 8, LANE), F32),
            pltpu.VMEM((2, 1, LANE), F32), pltpu.VMEM((ROWS, 1, LANE), F32), pltpu.VMEM((COLS, 1, LANE), F32),
            dma((3,)), dma((9,)), dma((9,)), dma((16,)), dma((16,)), dma, dma, dma, dma, pltpu.SemaphoreType.REGULAR((3,)),
        ],
        compiler_params=pltpu.CompilerParams(collective_id=0, has_side_effects=True, vmem_limit_bytes=20 * 2**20),
        name="gather",
    )(*(pltpu.with_memory_space_constraint(x, pltpu.HBM) for x in (coadd_flux, inverse_variance, source_mask)))
    return pl.pallas_call(
        blur_kernel,
        out_shape=[jax.ShapeDtypeStruct((H, W), F32)] * 2,
        in_specs=[vmem] * len(fields),
        out_specs=[vmem] * 2,
        compiler_params=pltpu.CompilerParams(vmem_limit_bytes=20 * 2**20),
        name="blur",
    )(*mids)


def solution(mesh):
    return jax.shard_map(
        block,
        mesh=mesh,
        in_specs=(P("rows", "cols"),) * 3,
        out_specs=(P("rows", "cols"),) * 2,
        check_vma=False,
    )
```

```python
import functools

import jax
import jax.numpy as jnp
import numpy as np
from jax import lax
from jax.experimental import pallas as pl
from jax.experimental.pallas import tpu as pltpu
from jax.sharding import PartitionSpec as P

RADIUS = 32
SIGMA = 10.0
SMOOTH = 2.0
REACH = 2 * RADIUS
ROWS, COLS = 32, 16
H, W = 128, 1024
HB = 72
LANE = 128
EW = W + 2 * LANE
BH = H + 2 * HB
SH, SW = H + 2 * REACH, W + 2 * REACH
MESH = pl.DeviceIdType.MESH
TAP_SUM = float(np.sum(np.exp(-np.arange(-RADIUS, RADIUS + 1) ** 2 / (2.0 * SIGMA * SIGMA))))
F32 = jnp.float32
BF16 = jnp.bfloat16


def tap(distance):
    d = distance.astype(F32)
    value = jnp.exp(-d * d / (2.0 * SIGMA * SIGMA)) / TAP_SUM
    return jnp.where(jnp.abs(distance) <= RADIUS, value, 0.0)


def iota(shape, dim):
    return lax.broadcasted_iota(jnp.int32, shape, dim)


def split(x):
    high = x.astype(BF16)
    return high, (x - high.astype(F32)).astype(BF16)


def dot32(a, b):
    return jnp.dot(a, b, precision=lax.Precision.HIGHEST, preferred_element_type=F32)


def total(x):
    return jnp.sum(jnp.sum(x, axis=0, keepdims=True), axis=1, keepdims=True)


def gather_kernel(
    f_hbm, iv_hbm, mk_hbm,
    fx, ux, vx, uc, vc, row_taps, col_taps, sums,
    fb, wb, ub, ivb, mkb, row_in, corner_in, col_out, col_in, msg, slots_p, slots_z,
    load_sem, near_send, near_recv, wide_send, wide_recv, p_send, p_recv, z_send, z_recv, chain,
):
    r, z = lax.axis_index("rows"), lax.axis_index("cols")
    r_up, r_dn = lax.rem(r + ROWS - 1, ROWS), lax.rem(r + 1, ROWS)
    z_lf, z_rt = lax.rem(z + COLS - 1, COLS), lax.rem(z + 1, COLS)
    has_up, has_dn, has_lf, has_rt = r > 0, r < ROWS - 1, z > 0, z < COLS - 1

    loads = [
        pltpu.make_async_copy(f_hbm, fb.at[pl.ds(HB, H), pl.ds(LANE, W)], load_sem.at[0]),
        pltpu.make_async_copy(iv_hbm, ivb, load_sem.at[1]),
        pltpu.make_async_copy(mk_hbm, mkb, load_sem.at[2]),
    ]
    for c in loads:
        c.start()
    barrier = pltpu.get_barrier_semaphore()
    count = 0
    for k in range(1, ROWS):
        pl.semaphore_signal(barrier, inc=1, device_id=(lax.rem(r + k, ROWS), z), device_id_type=MESH)
        count += 1
    for b in (z_lf, z_rt):
        pl.semaphore_signal(barrier, inc=1, device_id=(r, b), device_id_type=MESH)
        count += 1
    for a in (r_up, r_dn):
        for b in (z_lf, z_rt):
            pl.semaphore_signal(barrier, inc=1, device_id=(a, b), device_id_type=MESH)
            count += 1

    for c in loads:
        c.wait()

    def weigh(s, _):
        rows = pl.ds(pl.multiple_of(s * 8, 8), 8)
        there = pl.ds(pl.multiple_of(s * 8 + HB, 8), 8)
        w = ivb[rows, :] * (1.0 - mkb[rows, :].astype(F32))
        wb[there, LANE : LANE + W] = w
        uc[rows, :] = w * fb[there, LANE : LANE + W]
        return 0

    lax.fori_loop(0, H // 8, weigh, 0)
    col_out[0] = jnp.transpose(uc[:, 0:LANE])[0:8, :]
    col_out[1] = jnp.transpose(wb[HB : HB + H, LANE : 2 * LANE])[0:8, :]
    col_out[2] = jnp.transpose(uc[:, W - LANE : W])[LANE - 8 : LANE, :]

    pl.semaphore_wait(barrier, count)

    def entered(step):
        for away in (1 << step, COLS - (1 << step)):
            pl.semaphore_signal(chain.at[step], inc=1, device_id=(r, lax.rem(z + away, COLS)), device_id_type=MESH)

    entered(0)

    near = []

    def near_copy(src, dst, device, send_if, recv_if):
        k = len(near)
        c = pltpu.make_async_remote_copy(
            src_ref=src, dst_ref=dst, send_sem=near_send.at[k], recv_sem=near_recv.at[k],
            device_id=device, device_id_type=MESH,
        )
        near.append((c, send_if, recv_if))

    first, last = pl.ds(0, 8), pl.ds(H - 8, 8)
    mid, lf, rt = pl.ds(LANE, W), pl.ds(0, LANE), pl.ds(LANE + W, LANE)
    c_first, c_last = pl.ds(LANE, LANE), pl.ds(W, LANE)
    near_copy(uc.at[first], row_in.at[0], (r_up, z), has_up, has_dn)
    near_copy(wb.at[pl.ds(HB, 8), mid], row_in.at[1], (r_up, z), has_up, has_dn)
    near_copy(uc.at[last], row_in.at[2], (r_dn, z), has_dn, has_up)
    near_copy(col_out.at[0], col_in.at[0], (r, z_lf), has_lf, has_rt)
    near_copy(col_out.at[1], col_in.at[1], (r, z_lf), has_lf, has_rt)
    near_copy(col_out.at[2], col_in.at[2], (r, z_rt), has_rt, has_lf)
    block_lf, block_rt = pl.ds(0, LANE), pl.ds(W - LANE, LANE)
    near_copy(uc.at[last, block_lf], corner_in.at[0], (r_dn, z_lf), has_dn & has_lf, has_up & has_rt)
    near_copy(uc.at[first, block_lf], corner_in.at[1], (r_up, z_lf), has_up & has_lf, has_dn & has_rt)
    near_copy(uc.at[first, block_rt], corner_in.at[2], (r_up, z_rt), has_up & has_rt, has_dn & has_lf)
    for c, send_if, _ in near:
        pl.when(send_if)(c.start)
    wide = []

    def wide_copy(src_rows, src_cols, dst_rows, dst_cols, device, send_if, recv_if):
        for buf in (fb, wb):
            k = len(wide)
            c = pltpu.make_async_remote_copy(
                src_ref=buf.at[src_rows, src_cols], dst_ref=buf.at[dst_rows, dst_cols],
                send_sem=wide_send.at[k], recv_sem=wide_recv.at[k], device_id=device, device_id_type=MESH,
            )
            wide.append((c, send_if, recv_if))

    w_first, w_last, every = pl.ds(HB, HB), pl.ds(H, HB), pl.ds(HB, H)
    w_top, w_below = pl.ds(0, HB), pl.ds(HB + H, HB)
    wide_copy(every, c_first, every, rt, (r, z_lf), has_lf, has_rt)
    wide_copy(every, c_last, every, lf, (r, z_rt), has_rt, has_lf)
    wide_copy(w_first, mid, w_below, mid, (r_up, z), has_up, has_dn)
    wide_copy(w_last, mid, w_top, mid, (r_dn, z), has_dn, has_up)
    wide_copy(w_first, c_first, w_below, rt, (r_up, z_lf), has_up & has_lf, has_dn & has_rt)
    wide_copy(w_first, c_last, w_below, lf, (r_up, z_rt), has_up & has_rt, has_dn & has_lf)
    wide_copy(w_last, c_first, w_top, rt, (r_dn, z_lf), has_dn & has_lf, has_up & has_rt)
    wide_copy(w_last, c_last, w_top, lf, (r_dn, z_rt), has_dn & has_rt, has_up & has_lf)
    early = [n for n in range(len(wide)) if n not in (5, 7)]
    late = [5, 7]
    for n in early:
        pl.when(wide[n][1])(wide[n][0].start)

    cols8 = iota((8, EW), 1) - LANE
    rows8 = iota((8, EW), 0)

    def higher(src, row, x):
        before = src[pl.ds(pl.multiple_of(row - 8, 8), 8), :]
        return pltpu.roll(jnp.where(rows8 == 7, before, x), 1, 0)

    def lower(src, row, x):
        after = src[pl.ds(pl.multiple_of(row + 8, 8), 8), :]
        return pltpu.roll(jnp.where(rows8 == 0, after, x), 7, 0)

    def operator(src, row, u, w):
        above, under = higher(src, row, u), lower(src, row, u)
        beside = above + under + pltpu.roll(u, 1, 1) + pltpu.roll(u, EW - 1, 1)
        return w * u + SMOOTH * (4.0 * u - beside)

    rows_w, cols_w = iota((8, W), 0), iota((8, W), 1)
    lanes8 = iota((8, LANE), 1)

    def fold(x):
        x = jnp.sum(x.reshape(x.shape[0] // 8, 8, x.shape[1]), axis=0)
        return sum(x[:, c : c + LANE] for c in range(0, x.shape[1], LANE))

    def alone(s, acc):
        rows = pl.ds(pl.multiple_of(s * 8, 8), 8)
        u, w = uc[rows, :], wb[pl.ds(pl.multiple_of(s * 8 + HB, 8), 8), LANE : LANE + W]
        before = uc[pl.ds(pl.multiple_of(jnp.maximum(s - 1, 0) * 8, 8), 8), :]
        after = uc[pl.ds(pl.multiple_of(jnp.minimum(s + 1, H // 8 - 1) * 8, 8), 8), :]
        before = jnp.where(s > 0, before, 0.0)
        after = jnp.where(s < H // 8 - 1, after, 0.0)
        beside = pltpu.roll(jnp.where(rows_w == 7, before, u), 1, 0)
        beside = beside + pltpu.roll(jnp.where(rows_w == 0, after, u), 7, 0)
        beside = beside + pltpu.roll(jnp.where(cols_w == W - 1, 0.0, u), 1, 1)
        beside = beside + pltpu.roll(jnp.where(cols_w == 0, 0.0, u), W - 1, 1)
        vc[rows, :] = w * u + SMOOTH * (4.0 * u - beside)
        return acc + u * u

    uu = lax.fori_loop(0, H // 8, alone, jnp.zeros((8, W), F32))
    inner = W - 2 * LANE

    def terms_of(u, w, v, right, under, edge=None):
        vv = v * v
        curve = w * vv + SMOOTH * ((v - right) * (v - right) + (v - under) * (v - under))
        if edge is not None:
            curve = curve + SMOOTH * jnp.where(edge, vv, 0.0)
        return u * v, vv, curve

    def middle(s, acc):
        row = pl.multiple_of(s * 8, 8)
        rows, there = pl.ds(row, 8), pl.ds(pl.multiple_of(s * 8 + HB, 8), 8)
        v = vc[rows, LANE:W]
        right = pltpu.roll(v, inner + LANE - 1, 1)[:, 0:inner]
        v = v[:, 0:inner]
        after = vc[pl.ds(pl.multiple_of(s * 8 + 8, 8), 8), LANE : W - LANE]
        under = pltpu.roll(jnp.where(rows_w[:, 0:inner] == 0, after, v), 7, 0)
        t = terms_of(uc[rows, LANE : W - LANE], wb[there, 2 * LANE : W], v, right, under)
        return tuple(a + b for a, b in zip(acc, t))

    acc = lax.fori_loop(1, H // 8 - 1, middle, tuple(jnp.zeros((8, inner), F32) for _ in range(3)))
    sums4 = [fold(uu)] + [fold(a) for a in acc]

    pl.semaphore_wait(chain.at[0], 2)
    entered(1)
    for c, _, recv_if in near:
        pl.when(recv_if)(c.wait_recv)

    pad = jnp.zeros((LANE - 8, LANE), F32)

    def there(x, present):
        return jnp.where(present, x, jnp.zeros_like(x))

    top = there(row_in[2], has_up)
    below, below_w = there(row_in[0], has_dn), there(row_in[1], has_dn)
    cols_rt = jnp.transpose(jnp.concatenate([there(col_in[0], has_rt), pad], axis=0))
    cols_rt_w = jnp.transpose(jnp.concatenate([there(col_in[1], has_rt), pad], axis=0))
    cols_lf = jnp.transpose(jnp.concatenate([pad, there(col_in[2], has_lf)], axis=0))
    corner_up = there(corner_in[0], has_up & has_rt)[7:8, :]
    corner_dn = there(corner_in[1], has_dn & has_rt)
    corner_lf = there(corner_in[2], has_dn & has_lf)
    tile_rows, tile_cols = iota((H, LANE), 0), iota((H, LANE), 1)
    vc[0:8, :] -= SMOOTH * jnp.where(rows_w == 0, pltpu.roll(top, 1, 0), 0.0)
    vc[H - 8 : H, :] -= SMOOTH * jnp.where(rows_w == 7, pltpu.roll(below, 7, 0), 0.0)
    vc[:, 0:LANE] -= SMOOTH * jnp.where(tile_cols == 0, pltpu.roll(cols_lf, 1, 1), 0.0)
    vc[:, W - LANE : W] -= SMOOTH * jnp.where(tile_cols == LANE - 1, pltpu.roll(cols_rt, LANE - 1, 1), 0.0)

    beside = jnp.where(tile_rows == 0, corner_up, pltpu.roll(cols_rt, 1, 0))
    beside = beside + jnp.where(tile_rows == H - 1, corner_dn[0:1, :], pltpu.roll(cols_rt, H - 1, 0))
    beside = beside + pltpu.roll(uc[:, W - LANE : W], 1, 1) + pltpu.roll(cols_rt, LANE - 1, 1)
    v_rt = there(cols_rt_w * cols_rt + SMOOTH * (4.0 * cols_rt - beside), has_rt)

    line = jnp.concatenate([corner_lf, below, corner_dn], axis=1)
    beside = pltpu.roll(line, 1, 1)[:, LANE : LANE + W] + pltpu.roll(line, EW - 1, 1)[:, LANE : LANE + W]
    beside = beside + pltpu.roll(uc[H - 8 : H, :], 1, 0) + pltpu.roll(below, 7, 0)
    v_dn = there(below_w * below + SMOOTH * (4.0 * below - beside), has_dn)

    def ring(rows, cols, right, under, edge):
        here = wb[rows.start + HB : rows.stop + HB, cols.start + LANE : cols.stop + LANE]
        t = terms_of(uc[rows, cols], here, vc[rows, cols], right, under, edge)
        for k in range(3):
            sums4[k + 1] = sums4[k + 1] + fold(t[k])

    def shifted(x, beyond):
        x = jnp.concatenate([x, beyond], axis=1)
        return pltpu.roll(x, x.shape[1] - 1, 1)[:, 0 : x.shape[1] - LANE]

    every_col = slice(0, W)
    v = vc[0:8, :]
    edge = ((rows_w == 0) & (r == 0)).astype(F32) + ((cols_w == 0) & (z == 0)).astype(F32)
    ring(slice(0, 8), every_col, shifted(v, v_rt[0:8]), pltpu.roll(jnp.where(rows_w == 0, vc[8:16, :], v), 7, 0), None)
    sums4[3] = sums4[3] + SMOOTH * fold(edge * v * v)
    v = vc[H - 8 : H, :]
    ring(slice(H - 8, H), every_col, shifted(v, v_rt[H - 8 : H]), pltpu.roll(jnp.where(rows_w == 0, v_dn, v), 7, 0), (cols_w == 0) & (z == 0))
    body, body_next = slice(8, H - 8), slice(9, H - 7)
    first_cols, last_cols = slice(0, LANE), slice(W - LANE, W)
    at_left = (iota((H - 16, LANE), 1) == 0) & (z == 0)
    ring(body, first_cols, shifted(vc[body, first_cols], vc[body, LANE : 2 * LANE]), vc[body_next, first_cols], at_left)
    ring(body, last_cols, shifted(vc[body, last_cols], v_rt[8 : H - 8]), vc[body_next, last_cols], None)
    acc = sums4

    lane = iota((1, LANE), 1)
    packed = jnp.zeros((1, LANE), F32)
    for k, a in enumerate(acc):
        packed = jnp.where(lane == k, total(a), packed)
    msg[0] = packed

    def exchange(mine, slots, me, number, device, send_sem, recv_sem):
        copies = [
            pltpu.make_async_remote_copy(
                src_ref=mine, dst_ref=slots.at[me], send_sem=send_sem, recv_sem=recv_sem,
                device_id=device(lax.rem(me + k, number)), device_id_type=MESH,
            )
            for k in range(1, number)
        ]
        for c in copies:
            c.start()
        slots[me] = mine[...]

    def settle(slots, number, sems):
        arrivals = slots.at[pl.ds(0, number - 1)]
        for sem in sems:
            pltpu.make_async_copy(arrivals, arrivals, sem).wait()

    exchange(msg.at[0], slots_p, r, ROWS, lambda i: (i, z), p_send, p_recv)

    for n in late:
        pl.when(wide[n][1])(wide[n][0].start)
    pl.semaphore_wait(chain.at[1], 2)
    entered(2)
    def square(height, width):
        return iota((height, width), 0), iota((height, width), 1)

    i, k = square(H, 256)
    at = r * H - REACH + k
    one = jnp.where((at >= 0) & (at < ROWS * H), tap(k - REACH - i), 0.0)
    k, j = square(256, 256)
    high, low = split(dot32(one, tap(k - j)))
    row_taps[0:H, :] = high
    row_taps[H : 2 * H, :] = low
    for n, t in enumerate((0, 3, 7)):
        j, k = square(256, 256)
        at = z * W + t * LANE - REACH + k
        one = jnp.where((at >= 0) & (at < COLS * W), tap(j - k), 0.0)
        k, i = square(256, LANE)
        high, low = split(dot32(one, tap(k - REACH - i)))
        col_taps[n, :, 0:LANE] = high
        col_taps[n, :, LANE : 2 * LANE] = low

    settle(slots_p, ROWS, (p_send, p_recv))
    msg[1] = jnp.sum(slots_p[...], axis=0)
    pl.semaphore_wait(chain.at[2], 2)
    exchange(msg.at[1], slots_z, z, COLS, lambda i: (r, i), z_send, z_recv)

    for c, _, recv_if in wide:
        pl.when(recv_if)(c.wait_recv)

    def inside(row):
        at_row, at_col = rows8 + row + (r * H - HB), cols8 + z * W
        return (at_row >= 0) & (at_row < ROWS * H) & (at_col >= 0) & (at_col < COLS * W)

    def weighted(s, _):
        row = pl.multiple_of(s * 8, 8)
        here = pl.ds(row, 8)
        ub[here, :] = jnp.where(inside(row), fb[here, :] * wb[here, :], 0.0)
        return 0

    lax.fori_loop(0, BH // 8, weighted, 0)

    def extend(s, _):
        row = pl.multiple_of(s * 8 + 8, 8)
        here, there = pl.ds(row, 8), pl.ds(pl.multiple_of(s * 8, 8), 8)
        keep = inside(row)
        u = ub[here, :]
        v = jnp.where(keep, operator(ub, row, u, wb[here, :]), 0.0)
        f = jnp.where(keep, fb[here, :], 0.0)
        for dst, x in ((fx, f), (ux, u), (vx, v)):
            dst[there, :] = pltpu.roll(x, EW - (LANE - REACH), 1)[:, 0:SW]
        return 0

    lax.fori_loop(0, SH // 8, extend, 0)

    settle(slots_z, COLS, (z_send, z_recv))
    sums[...] = jnp.sum(slots_z[...], axis=0)

    for c, send_if, _ in near + wide:
        pl.when(send_if)(c.wait_send)


def blur_kernel(fx, ux, vx, uc, vc, row_taps, col_taps, sums, background, rms):
    g = sums[...]
    uu, uau, vv, vav = (g[0:1, k : k + 1] for k in range(4))
    alpha = uu / uau
    new = alpha * alpha * vv - uu
    keep = 1.0 + new / uu
    curve = keep * keep * uau - 2.0 * keep * alpha * vv + alpha * alpha * vav
    alpha1 = new / curve
    on_u = alpha + alpha1 * keep
    on_v = alpha1 * alpha
    background[...] = on_u * uc[...] - on_v * vc[...]
    taps_hl, taps_h = row_taps[...], row_taps[0:H, :]
    wide = SW // 2
    parts = []
    for start in (0, wide // LANE * LANE, SW):
        parts.append(start)
    highs, lows = [], []
    for a, b in zip(parts[:-1], parts[1:]):
        s = fx[:, a:b] - (on_u * ux[:, a:b] - on_v * vx[:, a:b])
        high, low = split(s * s)
        both = jnp.dot(taps_hl, high, preferred_element_type=F32)
        y = both[0:H] + both[H : 2 * H] + jnp.dot(taps_h, low, preferred_element_type=F32)
        high, low = split(y)
        highs.append(high)
        lows.append(low)
    yh, yl = jnp.concatenate(highs, axis=1), jnp.concatenate(lows, axis=1)
    for t in range(W // LANE):
        n = 0 if t == 0 else 2 if t == W // LANE - 1 else 1
        window = slice(t * LANE, t * LANE + 256)
        both = jnp.dot(yh[:, window], col_taps[n], preferred_element_type=F32)
        out = both[:, 0:LANE] + both[:, LANE:]
        out = out + jnp.dot(yl[:, window], col_taps[n, :, 0:LANE], preferred_element_type=F32)
        rms[:, t * LANE : (t + 1) * LANE] = jnp.sqrt(out + 1e-06)


def block(coadd_flux, inverse_variance, source_mask):
    vmem = pl.BlockSpec(memory_space=pltpu.VMEM)
    anywhere = pl.BlockSpec(memory_space=pltpu.HBM)
    fields = [jax.ShapeDtypeStruct((SH, SW), F32)] * 3 + [jax.ShapeDtypeStruct((H, W), F32)] * 2
    fields += [jax.ShapeDtypeStruct((2 * H, 256), BF16), jax.ShapeDtypeStruct((3, 256, 256), BF16)]
    fields += [jax.ShapeDtypeStruct((1, LANE), F32)]
    dma = pltpu.SemaphoreType.DMA
    mids = pl.pallas_call(
        gather_kernel,
        out_shape=fields,
        in_specs=[anywhere] * 3,
        out_specs=[vmem] * len(fields),
        scratch_shapes=[
            pltpu.VMEM((BH, EW), F32), pltpu.VMEM((BH, EW), F32), pltpu.VMEM((BH, EW), F32),
            pltpu.VMEM((H, W), F32), pltpu.VMEM((H, W), jnp.int32),
            pltpu.VMEM((3, 8, W), F32), pltpu.VMEM((3, 8, LANE), F32),
            pltpu.VMEM((3, 8, LANE), F32), pltpu.VMEM((3, 8, LANE), F32),
            pltpu.VMEM((2, 1, LANE), F32), pltpu.VMEM((ROWS, 1, LANE), F32), pltpu.VMEM((COLS, 1, LANE), F32),
            dma((3,)), dma((9,)), dma((9,)), dma((16,)), dma((16,)), dma, dma, dma, dma, pltpu.SemaphoreType.REGULAR((3,)),
        ],
        compiler_params=pltpu.CompilerParams(collective_id=0, has_side_effects=True, vmem_limit_bytes=20 * 2**20),
        name="gather",
    )(*(pltpu.with_memory_space_constraint(x, pltpu.HBM) for x in (coadd_flux, inverse_variance, source_mask)))
    return pl.pallas_call(
        blur_kernel,
        out_shape=[jax.ShapeDtypeStruct((H, W), F32)] * 2,
        in_specs=[vmem] * len(fields),
        out_specs=[vmem] * 2,
        compiler_params=pltpu.CompilerParams(vmem_limit_bytes=20 * 2**20),
        name="blur",
    )(*mids)


def solution(mesh):
    return jax.shard_map(
        block,
        mesh=mesh,
        in_specs=(P("rows", "cols"),) * 3,
        out_specs=(P("rows", "cols"),) * 2,
        check_vma=False,
    )
```

```python
import functools

import jax
import jax.numpy as jnp
import numpy as np
from jax import lax
from jax.experimental import pallas as pl
from jax.experimental.pallas import tpu as pltpu
from jax.sharding import PartitionSpec as P

RADIUS = 32
SIGMA = 10.0
SMOOTH = 2.0
REACH = 2 * RADIUS
ROWS, COLS = 32, 16
H, W = 128, 1024
HB = 72
LANE = 128
EW = W + 2 * LANE
BH = H + 2 * HB
SH, SW = H + 2 * REACH, W + 2 * REACH
MESH = pl.DeviceIdType.MESH
TAP_SUM = float(np.sum(np.exp(-np.arange(-RADIUS, RADIUS + 1) ** 2 / (2.0 * SIGMA * SIGMA))))
PLANE_ORDER = sorted(range(1, ROWS), key=lambda k: -min(k // 8, 4 - k // 8) - min(k % 8 // 2, 4 - k % 8 // 2))
COLUMN_ORDER = sorted(range(1, COLS), key=lambda k: -min(k, COLS - k))
F32 = jnp.float32
BF16 = jnp.bfloat16


def tap(distance):
    d = distance.astype(F32)
    value = jnp.exp(-d * d / (2.0 * SIGMA * SIGMA)) / TAP_SUM
    return jnp.where(jnp.abs(distance) <= RADIUS, value, 0.0)


def iota(shape, dim):
    return lax.broadcasted_iota(jnp.int32, shape, dim)


def split(x):
    high = x.astype(BF16)
    return high, (x - high.astype(F32)).astype(BF16)


def dot32(a, b):
    return jnp.dot(a, b, precision=lax.Precision.HIGHEST, preferred_element_type=F32)


def total(x):
    return jnp.sum(jnp.sum(x, axis=0, keepdims=True), axis=1, keepdims=True)


def gather_kernel(
    f_hbm, iv_hbm, mk_hbm,
    fx, ux, vx, uc, vc, row_taps, col_taps, sums,
    fb, wb, ub, ivb, mkb, row_in, corner_in, col_out, col_in, msg, slots_p, slots_z,
    load_sem, near_send, near_recv, wide_send, wide_recv, p_send, p_recv, z_send, z_recv, chain,
):
    r, z = lax.axis_index("rows"), lax.axis_index("cols")
    r_up, r_dn = lax.rem(r + ROWS - 1, ROWS), lax.rem(r + 1, ROWS)
    z_lf, z_rt = lax.rem(z + COLS - 1, COLS), lax.rem(z + 1, COLS)
    has_up, has_dn, has_lf, has_rt = r > 0, r < ROWS - 1, z > 0, z < COLS - 1

    loads = [
        pltpu.make_async_copy(f_hbm, fb.at[pl.ds(HB, H), pl.ds(LANE, W)], load_sem.at[0]),
        pltpu.make_async_copy(iv_hbm, ivb, load_sem.at[1]),
        pltpu.make_async_copy(mk_hbm, mkb, load_sem.at[2]),
    ]
    for c in loads:
        c.start()
    barrier = pltpu.get_barrier_semaphore()
    count = 0
    for a in (r_up, r_dn):
        for b in (z_lf, z_rt):
            pl.semaphore_signal(barrier, inc=1, device_id=(a, b), device_id_type=MESH)
            count += 1
    for k in PLANE_ORDER:
        pl.semaphore_signal(barrier, inc=1, device_id=(lax.rem(r + k, ROWS), z), device_id_type=MESH)
        count += 1
    for b in (z_lf, z_rt):
        pl.semaphore_signal(barrier, inc=1, device_id=(r, b), device_id_type=MESH)
        count += 1

    for c in loads:
        c.wait()

    def weigh(s, _):
        rows = pl.ds(pl.multiple_of(s * 8, 8), 8)
        there = pl.ds(pl.multiple_of(s * 8 + HB, 8), 8)
        w = ivb[rows, :] * (1.0 - mkb[rows, :].astype(F32))
        wb[there, LANE : LANE + W] = w
        uc[rows, :] = w * fb[there, LANE : LANE + W]
        return 0

    lax.fori_loop(0, H // 8, weigh, 0)
    col_out[0] = jnp.transpose(uc[:, 0:LANE])[0:8, :]
    col_out[1] = jnp.transpose(wb[HB : HB + H, LANE : 2 * LANE])[0:8, :]
    col_out[2] = jnp.transpose(uc[:, W - LANE : W])[LANE - 8 : LANE, :]

    pl.semaphore_wait(barrier, count)

    def entered(step):
        for away in (1 << step, COLS - (1 << step)):
            pl.semaphore_signal(chain.at[step], inc=1, device_id=(r, lax.rem(z + away, COLS)), device_id_type=MESH)

    entered(0)

    near = []

    def near_copy(src, dst, device, send_if, recv_if):
        k = len(near)
        c = pltpu.make_async_remote_copy(
            src_ref=src, dst_ref=dst, send_sem=near_send.at[k], recv_sem=near_recv.at[k],
            device_id=device, device_id_type=MESH,
        )
        near.append((c, send_if, recv_if))

    first, last = pl.ds(0, 8), pl.ds(H - 8, 8)
    mid, lf, rt = pl.ds(LANE, W), pl.ds(0, LANE), pl.ds(LANE + W, LANE)
    c_first, c_last = pl.ds(LANE, LANE), pl.ds(W, LANE)
    near_copy(uc.at[first], row_in.at[0], (r_up, z), has_up, has_dn)
    near_copy(wb.at[pl.ds(HB, 8), mid], row_in.at[1], (r_up, z), has_up, has_dn)
    near_copy(uc.at[last], row_in.at[2], (r_dn, z), has_dn, has_up)
    near_copy(col_out.at[0], col_in.at[0], (r, z_lf), has_lf, has_rt)
    near_copy(col_out.at[1], col_in.at[1], (r, z_lf), has_lf, has_rt)
    near_copy(col_out.at[2], col_in.at[2], (r, z_rt), has_rt, has_lf)
    block_lf, block_rt = pl.ds(0, LANE), pl.ds(W - LANE, LANE)
    near_copy(uc.at[last, block_lf], corner_in.at[0], (r_dn, z_lf), has_dn & has_lf, has_up & has_rt)
    near_copy(uc.at[first, block_lf], corner_in.at[1], (r_up, z_lf), has_up & has_lf, has_dn & has_rt)
    near_copy(uc.at[first, block_rt], corner_in.at[2], (r_up, z_rt), has_up & has_rt, has_dn & has_lf)
    for c, send_if, _ in near:
        pl.when(send_if)(c.start)
    wide = []

    def wide_copy(src_rows, src_cols, dst_rows, dst_cols, device, send_if, recv_if):
        for buf in (fb, wb):
            k = len(wide)
            c = pltpu.make_async_remote_copy(
                src_ref=buf.at[src_rows, src_cols], dst_ref=buf.at[dst_rows, dst_cols],
                send_sem=wide_send.at[k], recv_sem=wide_recv.at[k], device_id=device, device_id_type=MESH,
            )
            wide.append((c, send_if, recv_if))

    w_first, w_last, every = pl.ds(HB, HB), pl.ds(H, HB), pl.ds(HB, H)
    w_top, w_below = pl.ds(0, HB), pl.ds(HB + H, HB)
    wide_copy(every, c_first, every, rt, (r, z_lf), has_lf, has_rt)
    wide_copy(every, c_last, every, lf, (r, z_rt), has_rt, has_lf)
    wide_copy(w_first, mid, w_below, mid, (r_up, z), has_up, has_dn)
    wide_copy(w_last, mid, w_top, mid, (r_dn, z), has_dn, has_up)
    wide_copy(w_first, c_first, w_below, rt, (r_up, z_lf), has_up & has_lf, has_dn & has_rt)
    wide_copy(w_first, c_last, w_below, lf, (r_up, z_rt), has_up & has_rt, has_dn & has_lf)
    wide_copy(w_last, c_first, w_top, rt, (r_dn, z_lf), has_dn & has_lf, has_up & has_rt)
    wide_copy(w_last, c_last, w_top, lf, (r_dn, z_rt), has_dn & has_rt, has_up & has_lf)
    early = [n for n in range(len(wide)) if n not in (5, 7)]
    late = [5, 7]
    for n in early:
        pl.when(wide[n][1])(wide[n][0].start)

    cols8 = iota((8, EW), 1) - LANE
    rows8 = iota((8, EW), 0)

    def higher(src, row, x):
        before = src[pl.ds(pl.multiple_of(row - 8, 8), 8), :]
        return pltpu.roll(jnp.where(rows8 == 7, before, x), 1, 0)

    def lower(src, row, x):
        after = src[pl.ds(pl.multiple_of(row + 8, 8), 8), :]
        return pltpu.roll(jnp.where(rows8 == 0, after, x), 7, 0)

    def operator(src, row, u, w):
        above, under = higher(src, row, u), lower(src, row, u)
        beside = above + under + pltpu.roll(u, 1, 1) + pltpu.roll(u, EW - 1, 1)
        return w * u + SMOOTH * (4.0 * u - beside)

    rows_w, cols_w = iota((8, W), 0), iota((8, W), 1)
    lanes8 = iota((8, LANE), 1)

    def fold(x):
        x = jnp.sum(x.reshape(x.shape[0] // 8, 8, x.shape[1]), axis=0)
        return sum(x[:, c : c + LANE] for c in range(0, x.shape[1], LANE))

    def alone(s, acc):
        rows = pl.ds(pl.multiple_of(s * 8, 8), 8)
        u, w = uc[rows, :], wb[pl.ds(pl.multiple_of(s * 8 + HB, 8), 8), LANE : LANE + W]
        before = uc[pl.ds(pl.multiple_of(jnp.maximum(s - 1, 0) * 8, 8), 8), :]
        after = uc[pl.ds(pl.multiple_of(jnp.minimum(s + 1, H // 8 - 1) * 8, 8), 8), :]
        before = jnp.where(s > 0, before, 0.0)
        after = jnp.where(s < H // 8 - 1, after, 0.0)
        beside = pltpu.roll(jnp.where(rows_w == 7, before, u), 1, 0)
        beside = beside + pltpu.roll(jnp.where(rows_w == 0, after, u), 7, 0)
        beside = beside + pltpu.roll(jnp.where(cols_w == W - 1, 0.0, u), 1, 1)
        beside = beside + pltpu.roll(jnp.where(cols_w == 0, 0.0, u), W - 1, 1)
        vc[rows, :] = w * u + SMOOTH * (4.0 * u - beside)
        return acc + u * u

    uu = lax.fori_loop(0, H // 8, alone, jnp.zeros((8, W), F32))
    inner = W - 2 * LANE

    def terms_of(u, w, v, right, under, edge=None):
        vv = v * v
        curve = w * vv + SMOOTH * ((v - right) * (v - right) + (v - under) * (v - under))
        if edge is not None:
            curve = curve + SMOOTH * jnp.where(edge, vv, 0.0)
        return u * v, vv, curve

    def middle(s, acc):
        row = pl.multiple_of(s * 8, 8)
        rows, there = pl.ds(row, 8), pl.ds(pl.multiple_of(s * 8 + HB, 8), 8)
        v = vc[rows, LANE:W]
        right = pltpu.roll(v, inner + LANE - 1, 1)[:, 0:inner]
        v = v[:, 0:inner]
        after = vc[pl.ds(pl.multiple_of(s * 8 + 8, 8), 8), LANE : W - LANE]
        under = pltpu.roll(jnp.where(rows_w[:, 0:inner] == 0, after, v), 7, 0)
        t = terms_of(uc[rows, LANE : W - LANE], wb[there, 2 * LANE : W], v, right, under)
        return tuple(a + b for a, b in zip(acc, t))

    acc = lax.fori_loop(1, H // 8 - 1, middle, tuple(jnp.zeros((8, inner), F32) for _ in range(3)))
    sums4 = [fold(uu)] + [fold(a) for a in acc]

    pl.semaphore_wait(chain.at[0], 2)
    entered(1)
    for c, _, recv_if in near:
        pl.when(recv_if)(c.wait_recv)

    pad = jnp.zeros((LANE - 8, LANE), F32)

    def there(x, present):
        return jnp.where(present, x, jnp.zeros_like(x))

    top = there(row_in[2], has_up)
    below, below_w = there(row_in[0], has_dn), there(row_in[1], has_dn)
    cols_rt = jnp.transpose(jnp.concatenate([there(col_in[0], has_rt), pad], axis=0))
    cols_rt_w = jnp.transpose(jnp.concatenate([there(col_in[1], has_rt), pad], axis=0))
    cols_lf = jnp.transpose(jnp.concatenate([pad, there(col_in[2], has_lf)], axis=0))
    corner_up = there(corner_in[0], has_up & has_rt)[7:8, :]
    corner_dn = there(corner_in[1], has_dn & has_rt)
    corner_lf = there(corner_in[2], has_dn & has_lf)
    tile_rows, tile_cols = iota((H, LANE), 0), iota((H, LANE), 1)
    vc[0:8, :] -= SMOOTH * jnp.where(rows_w == 0, pltpu.roll(top, 1, 0), 0.0)
    vc[H - 8 : H, :] -= SMOOTH * jnp.where(rows_w == 7, pltpu.roll(below, 7, 0), 0.0)
    vc[:, 0:LANE] -= SMOOTH * jnp.where(tile_cols == 0, pltpu.roll(cols_lf, 1, 1), 0.0)
    vc[:, W - LANE : W] -= SMOOTH * jnp.where(tile_cols == LANE - 1, pltpu.roll(cols_rt, LANE - 1, 1), 0.0)

    beside = jnp.where(tile_rows == 0, corner_up, pltpu.roll(cols_rt, 1, 0))
    beside = beside + jnp.where(tile_rows == H - 1, corner_dn[0:1, :], pltpu.roll(cols_rt, H - 1, 0))
    beside = beside + pltpu.roll(uc[:, W - LANE : W], 1, 1) + pltpu.roll(cols_rt, LANE - 1, 1)
    v_rt = there(cols_rt_w * cols_rt + SMOOTH * (4.0 * cols_rt - beside), has_rt)

    line = jnp.concatenate([corner_lf, below, corner_dn], axis=1)
    beside = pltpu.roll(line, 1, 1)[:, LANE : LANE + W] + pltpu.roll(line, EW - 1, 1)[:, LANE : LANE + W]
    beside = beside + pltpu.roll(uc[H - 8 : H, :], 1, 0) + pltpu.roll(below, 7, 0)
    v_dn = there(below_w * below + SMOOTH * (4.0 * below - beside), has_dn)

    def ring(rows, cols, right, under, edge):
        here = wb[rows.start + HB : rows.stop + HB, cols.start + LANE : cols.stop + LANE]
        t = terms_of(uc[rows, cols], here, vc[rows, cols], right, under, edge)
        for k in range(3):
            sums4[k + 1] = sums4[k + 1] + fold(t[k])

    def shifted(x, beyond):
        x = jnp.concatenate([x, beyond], axis=1)
        return pltpu.roll(x, x.shape[1] - 1, 1)[:, 0 : x.shape[1] - LANE]

    every_col = slice(0, W)
    v = vc[0:8, :]
    edge = ((rows_w == 0) & (r == 0)).astype(F32) + ((cols_w == 0) & (z == 0)).astype(F32)
    ring(slice(0, 8), every_col, shifted(v, v_rt[0:8]), pltpu.roll(jnp.where(rows_w == 0, vc[8:16, :], v), 7, 0), None)
    sums4[3] = sums4[3] + SMOOTH * fold(edge * v * v)
    v = vc[H - 8 : H, :]
    ring(slice(H - 8, H), every_col, shifted(v, v_rt[H - 8 : H]), pltpu.roll(jnp.where(rows_w == 0, v_dn, v), 7, 0), (cols_w == 0) & (z == 0))
    body, body_next = slice(8, H - 8), slice(9, H - 7)
    first_cols, last_cols = slice(0, LANE), slice(W - LANE, W)
    at_left = (iota((H - 16, LANE), 1) == 0) & (z == 0)
    ring(body, first_cols, shifted(vc[body, first_cols], vc[body, LANE : 2 * LANE]), vc[body_next, first_cols], at_left)
    ring(body, last_cols, shifted(vc[body, last_cols], v_rt[8 : H - 8]), vc[body_next, last_cols], None)
    acc = sums4

    lane = iota((1, LANE), 1)
    packed = jnp.zeros((1, LANE), F32)
    for k, a in enumerate(acc):
        packed = jnp.where(lane == k, total(a), packed)
    msg[0] = packed

    def exchange(mine, slots, me, number, device, send_sem, recv_sem):
        copies = [
            pltpu.make_async_remote_copy(
                src_ref=mine, dst_ref=slots.at[me], send_sem=send_sem, recv_sem=recv_sem,
                device_id=device(lax.rem(me + k, number)), device_id_type=MESH,
            )
            for k in (PLANE_ORDER if number == ROWS else COLUMN_ORDER)
        ]
        for c in copies:
            c.start()
        slots[me] = mine[...]

    def settle(slots, number, sems):
        arrivals = slots.at[pl.ds(0, number - 1)]
        for sem in sems:
            pltpu.make_async_copy(arrivals, arrivals, sem).wait()

    exchange(msg.at[0], slots_p, r, ROWS, lambda i: (i, z), p_send, p_recv)

    for n in late:
        pl.when(wide[n][1])(wide[n][0].start)
    pl.semaphore_wait(chain.at[1], 2)
    entered(2)
    def square(height, width):
        return iota((height, width), 0), iota((height, width), 1)

    i, k = square(H, 256)
    at = r * H - REACH + k
    one = jnp.where((at >= 0) & (at < ROWS * H), tap(k - REACH - i), 0.0)
    k, j = square(256, 256)
    high, low = split(dot32(one, tap(k - j)))
    row_taps[0:H, :] = high
    row_taps[H : 2 * H, :] = low
    for n, t in enumerate((0, 3, 7)):
        j, k = square(256, 256)
        at = z * W + t * LANE - REACH + k
        one = jnp.where((at >= 0) & (at < COLS * W), tap(j - k), 0.0)
        k, i = square(256, LANE)
        high, low = split(dot32(one, tap(k - REACH - i)))
        col_taps[n, :, 0:LANE] = high
        col_taps[n, :, LANE : 2 * LANE] = low

    settle(slots_p, ROWS, (p_send, p_recv))
    msg[1] = jnp.sum(slots_p[...], axis=0)
    pl.semaphore_wait(chain.at[2], 2)
    exchange(msg.at[1], slots_z, z, COLS, lambda i: (r, i), z_send, z_recv)

    for c, _, recv_if in wide:
        pl.when(recv_if)(c.wait_recv)

    def inside(row):
        at_row, at_col = rows8 + row + (r * H - HB), cols8 + z * W
        return (at_row >= 0) & (at_row < ROWS * H) & (at_col >= 0) & (at_col < COLS * W)

    def weighted(s, _):
        row = pl.multiple_of(s * 8, 8)
        here = pl.ds(row, 8)
        ub[here, :] = jnp.where(inside(row), fb[here, :] * wb[here, :], 0.0)
        return 0

    lax.fori_loop(0, BH // 8, weighted, 0)

    def extend(s, _):
        row = pl.multiple_of(s * 8 + 8, 8)
        here, there = pl.ds(row, 8), pl.ds(pl.multiple_of(s * 8, 8), 8)
        keep = inside(row)
        u = ub[here, :]
        v = jnp.where(keep, operator(ub, row, u, wb[here, :]), 0.0)
        f = jnp.where(keep, fb[here, :], 0.0)
        for dst, x in ((fx, f), (ux, u), (vx, v)):
            dst[there, :] = pltpu.roll(x, EW - (LANE - REACH), 1)[:, 0:SW]
        return 0

    lax.fori_loop(0, SH // 8, extend, 0)

    settle(slots_z, COLS, (z_send, z_recv))
    sums[...] = jnp.sum(slots_z[...], axis=0)

    for c, send_if, _ in near + wide:
        pl.when(send_if)(c.wait_send)


def blur_kernel(fx, ux, vx, uc, vc, row_taps, col_taps, sums, background, rms, field, scatter, sem):
    g = sums[...]
    uu, uau, vv, vav = (g[0:1, k : k + 1] for k in range(4))
    alpha = uu / uau
    new = alpha * alpha * vv - uu
    keep = 1.0 + new / uu
    curve = keep * keep * uau - 2.0 * keep * alpha * vv + alpha * alpha * vav
    alpha1 = new / curve
    on_u = alpha + alpha1 * keep
    on_v = alpha1 * alpha
    field[...] = on_u * uc[...] - on_v * vc[...]
    writes = [pltpu.make_async_copy(field, background, sem.at[0])]
    writes[0].start()
    taps_hl, taps_h = row_taps[...], row_taps[0:H, :]
    wide = SW // 2
    parts = []
    for start in (0, wide // LANE * LANE, SW):
        parts.append(start)
    highs, lows = [], []
    for a, b in zip(parts[:-1], parts[1:]):
        s = fx[:, a:b] - (on_u * ux[:, a:b] - on_v * vx[:, a:b])
        high, low = split(s * s)
        both = jnp.dot(taps_hl, high, preferred_element_type=F32)
        y = both[0:H] + both[H : 2 * H] + jnp.dot(taps_h, low, preferred_element_type=F32)
        high, low = split(y)
        highs.append(high)
        lows.append(low)
    yh, yl = jnp.concatenate(highs, axis=1), jnp.concatenate(lows, axis=1)
    for t in range(W // LANE):
        n = 0 if t == 0 else 2 if t == W // LANE - 1 else 1
        window = slice(t * LANE, t * LANE + 256)
        both = jnp.dot(yh[:, window], col_taps[n], preferred_element_type=F32)
        out = both[:, 0:LANE] + both[:, LANE:]
        out = out + jnp.dot(yl[:, window], col_taps[n, :, 0:LANE], preferred_element_type=F32)
        scatter[:, t * LANE : (t + 1) * LANE] = jnp.sqrt(out + 1e-06)
        if t % 2:
            pair = pl.ds((t - 1) * LANE, 2 * LANE)
            writes.append(pltpu.make_async_copy(scatter.at[:, pair], rms.at[:, pair], sem.at[1 + t // 2]))
            writes[-1].start()
    for c in writes:
        c.wait()


def block(coadd_flux, inverse_variance, source_mask):
    vmem = pl.BlockSpec(memory_space=pltpu.VMEM)
    anywhere = pl.BlockSpec(memory_space=pltpu.HBM)
    fields = [jax.ShapeDtypeStruct((SH, SW), F32)] * 3 + [jax.ShapeDtypeStruct((H, W), F32)] * 2
    fields += [jax.ShapeDtypeStruct((2 * H, 256), BF16), jax.ShapeDtypeStruct((3, 256, 256), BF16)]
    fields += [jax.ShapeDtypeStruct((1, LANE), F32)]
    dma = pltpu.SemaphoreType.DMA
    mids = pl.pallas_call(
        gather_kernel,
        out_shape=fields,
        in_specs=[anywhere] * 3,
        out_specs=[vmem] * len(fields),
        scratch_shapes=[
            pltpu.VMEM((BH, EW), F32), pltpu.VMEM((BH, EW), F32), pltpu.VMEM((BH, EW), F32),
            pltpu.VMEM((H, W), F32), pltpu.VMEM((H, W), jnp.int32),
            pltpu.VMEM((3, 8, W), F32), pltpu.VMEM((3, 8, LANE), F32),
            pltpu.VMEM((3, 8, LANE), F32), pltpu.VMEM((3, 8, LANE), F32),
            pltpu.VMEM((2, 1, LANE), F32), pltpu.VMEM((ROWS, 1, LANE), F32), pltpu.VMEM((COLS, 1, LANE), F32),
            dma((3,)), dma((9,)), dma((9,)), dma((16,)), dma((16,)), dma, dma, dma, dma, pltpu.SemaphoreType.REGULAR((3,)),
        ],
        compiler_params=pltpu.CompilerParams(collective_id=0, has_side_effects=True, vmem_limit_bytes=20 * 2**20),
        name="gather",
    )(*(pltpu.with_memory_space_constraint(x, pltpu.HBM) for x in (coadd_flux, inverse_variance, source_mask)))
    return pl.pallas_call(
        blur_kernel,
        out_shape=[jax.ShapeDtypeStruct((H, W), F32)] * 2,
        in_specs=[vmem] * len(fields),
        out_specs=[anywhere] * 2,
        scratch_shapes=[pltpu.VMEM((H, W), F32), pltpu.VMEM((H, W), F32), pltpu.SemaphoreType.DMA((1 + W // LANE // 2,))],
        compiler_params=pltpu.CompilerParams(vmem_limit_bytes=20 * 2**20),
        name="blur",
    )(*mids)


def solution(mesh):
    return jax.shard_map(
        block,
        mesh=mesh,
        in_specs=(P("rows", "cols"),) * 3,
        out_specs=(P("rows", "cols"),) * 2,
        check_vma=False,
    )
```

```python
import functools

import jax
import jax.numpy as jnp
import numpy as np
from jax import lax
from jax.experimental import pallas as pl
from jax.experimental.pallas import tpu as pltpu
from jax.sharding import PartitionSpec as P

RADIUS = 32
SIGMA = 10.0
SMOOTH = 2.0
REACH = 2 * RADIUS
ROWS, COLS = 32, 16
H, W = 128, 1024
HB = 72
LANE = 128
EW = W + 2 * LANE
BH = H + 2 * HB
SH, SW = H + 2 * REACH, W + 2 * REACH
MESH = pl.DeviceIdType.MESH
TAP_SUM = float(np.sum(np.exp(-np.arange(-RADIUS, RADIUS + 1) ** 2 / (2.0 * SIGMA * SIGMA))))
PLANE_ORDER = sorted(range(1, ROWS), key=lambda k: -min(k // 8, 4 - k // 8) - min(k % 8 // 2, 4 - k % 8 // 2))
COLUMN_ORDER = sorted(range(1, COLS), key=lambda k: -min(k, COLS - k))
F32 = jnp.float32
BF16 = jnp.bfloat16


def tap(distance):
    d = distance.astype(F32)
    value = jnp.exp(-d * d / (2.0 * SIGMA * SIGMA)) / TAP_SUM
    return jnp.where(jnp.abs(distance) <= RADIUS, value, 0.0)


def iota(shape, dim):
    return lax.broadcasted_iota(jnp.int32, shape, dim)


def split(x):
    high = x.astype(BF16)
    return high, (x - high.astype(F32)).astype(BF16)


def dot32(a, b):
    return jnp.dot(a, b, precision=lax.Precision.HIGHEST, preferred_element_type=F32)


def total(x):
    return jnp.sum(jnp.sum(x, axis=0, keepdims=True), axis=1, keepdims=True)


def gather_kernel(
    f_hbm, iv_hbm, mk_hbm,
    fx, ux, vx, uc, vc, row_taps, col_taps, sums,
    fb, wb, ub, ivb, mkb, scaled, row_in, corner_in, col_out, col_in, msg, slots_p, slots_z,
    load_sem, near_send, near_recv, wide_send, wide_recv, p_send, p_recv, z_send, z_recv, chain,
):
    r, z = lax.axis_index("rows"), lax.axis_index("cols")
    r_up, r_dn = lax.rem(r + ROWS - 1, ROWS), lax.rem(r + 1, ROWS)
    z_lf, z_rt = lax.rem(z + COLS - 1, COLS), lax.rem(z + 1, COLS)
    has_up, has_dn, has_lf, has_rt = r > 0, r < ROWS - 1, z > 0, z < COLS - 1

    loads = [
        pltpu.make_async_copy(f_hbm, fb.at[pl.ds(HB, H), pl.ds(LANE, W)], load_sem.at[0]),
        pltpu.make_async_copy(iv_hbm, ivb, load_sem.at[1]),
        pltpu.make_async_copy(mk_hbm, mkb, load_sem.at[2]),
    ]
    for c in loads:
        c.start()
    barrier = pltpu.get_barrier_semaphore()
    count = 0
    for a in (r_up, r_dn):
        for b in (z_lf, z_rt):
            pl.semaphore_signal(barrier, inc=1, device_id=(a, b), device_id_type=MESH)
            count += 1
    for k in PLANE_ORDER:
        pl.semaphore_signal(barrier, inc=1, device_id=(lax.rem(r + k, ROWS), z), device_id_type=MESH)
        count += 1
    for b in (z_lf, z_rt):
        pl.semaphore_signal(barrier, inc=1, device_id=(r, b), device_id_type=MESH)
        count += 1

    for c in loads:
        c.wait()

    def weigh(s, _):
        rows = pl.ds(pl.multiple_of(s * 8, 8), 8)
        there = pl.ds(pl.multiple_of(s * 8 + HB, 8), 8)
        w = ivb[rows, :] * (1.0 - mkb[rows, :].astype(F32))
        wb[there, LANE : LANE + W] = w
        uc[rows, :] = w * fb[there, LANE : LANE + W]
        return 0

    lax.fori_loop(0, H // 8, weigh, 0)
    col_out[0] = jnp.transpose(uc[:, 0:LANE])[0:8, :]
    col_out[1] = jnp.transpose(wb[HB : HB + H, LANE : 2 * LANE])[0:8, :]
    col_out[2] = jnp.transpose(uc[:, W - LANE : W])[LANE - 8 : LANE, :]

    pl.semaphore_wait(barrier, count)

    def entered(step):
        for away in (1 << step, COLS - (1 << step)):
            pl.semaphore_signal(chain.at[step], inc=1, device_id=(r, lax.rem(z + away, COLS)), device_id_type=MESH)

    entered(0)

    near = []

    def near_copy(src, dst, device, send_if, recv_if):
        k = len(near)
        c = pltpu.make_async_remote_copy(
            src_ref=src, dst_ref=dst, send_sem=near_send.at[k], recv_sem=near_recv.at[k],
            device_id=device, device_id_type=MESH,
        )
        near.append((c, send_if, recv_if))

    first, last = pl.ds(0, 8), pl.ds(H - 8, 8)
    mid, lf, rt = pl.ds(LANE, W), pl.ds(0, LANE), pl.ds(LANE + W, LANE)
    c_first, c_last = pl.ds(LANE, LANE), pl.ds(W, LANE)
    near_copy(uc.at[first], row_in.at[0], (r_up, z), has_up, has_dn)
    near_copy(wb.at[pl.ds(HB, 8), mid], row_in.at[1], (r_up, z), has_up, has_dn)
    near_copy(uc.at[last], row_in.at[2], (r_dn, z), has_dn, has_up)
    near_copy(col_out.at[0], col_in.at[0], (r, z_lf), has_lf, has_rt)
    near_copy(col_out.at[1], col_in.at[1], (r, z_lf), has_lf, has_rt)
    near_copy(col_out.at[2], col_in.at[2], (r, z_rt), has_rt, has_lf)
    block_lf, block_rt = pl.ds(0, LANE), pl.ds(W - LANE, LANE)
    near_copy(uc.at[last, block_lf], corner_in.at[0], (r_dn, z_lf), has_dn & has_lf, has_up & has_rt)
    near_copy(uc.at[first, block_lf], corner_in.at[1], (r_up, z_lf), has_up & has_lf, has_dn & has_rt)
    near_copy(uc.at[first, block_rt], corner_in.at[2], (r_up, z_rt), has_up & has_rt, has_dn & has_lf)
    for c, send_if, _ in near:
        pl.when(send_if)(c.start)
    wide = []

    def wide_copy(src_rows, src_cols, dst_rows, dst_cols, device, send_if, recv_if):
        for buf in (fb, wb):
            k = len(wide)
            c = pltpu.make_async_remote_copy(
                src_ref=buf.at[src_rows, src_cols], dst_ref=buf.at[dst_rows, dst_cols],
                send_sem=wide_send.at[k], recv_sem=wide_recv.at[k], device_id=device, device_id_type=MESH,
            )
            wide.append((c, send_if, recv_if))

    w_first, w_last, every = pl.ds(HB, HB), pl.ds(H, HB), pl.ds(HB, H)
    w_top, w_below = pl.ds(0, HB), pl.ds(HB + H, HB)
    wide_copy(every, c_first, every, rt, (r, z_lf), has_lf, has_rt)
    wide_copy(every, c_last, every, lf, (r, z_rt), has_rt, has_lf)
    wide_copy(w_first, mid, w_below, mid, (r_up, z), has_up, has_dn)
    wide_copy(w_last, mid, w_top, mid, (r_dn, z), has_dn, has_up)
    wide_copy(w_first, c_first, w_below, rt, (r_up, z_lf), has_up & has_lf, has_dn & has_rt)
    wide_copy(w_first, c_last, w_below, lf, (r_up, z_rt), has_up & has_rt, has_dn & has_lf)
    wide_copy(w_last, c_first, w_top, rt, (r_dn, z_lf), has_dn & has_lf, has_up & has_rt)
    wide_copy(w_last, c_last, w_top, lf, (r_dn, z_rt), has_dn & has_rt, has_up & has_lf)
    early = [n for n in range(len(wide)) if n not in (5, 7)]
    late = [5, 7]
    for n in early:
        pl.when(wide[n][1])(wide[n][0].start)

    cols8 = iota((8, EW), 1) - LANE
    rows8 = iota((8, EW), 0)

    def higher(src, row, x):
        before = src[pl.ds(pl.multiple_of(row - 8, 8), 8), :]
        return pltpu.roll(jnp.where(rows8 == 7, before, x), 1, 0)

    def lower(src, row, x):
        after = src[pl.ds(pl.multiple_of(row + 8, 8), 8), :]
        return pltpu.roll(jnp.where(rows8 == 0, after, x), 7, 0)

    def operator(src, row, u, w):
        above, under = higher(src, row, u), lower(src, row, u)
        beside = above + under + pltpu.roll(u, 1, 1) + pltpu.roll(u, EW - 1, 1)
        return w * u + SMOOTH * (4.0 * u - beside)

    rows_w, cols_w = iota((8, W), 0), iota((8, W), 1)
    lanes8 = iota((8, LANE), 1)

    def fold(x):
        x = jnp.sum(x.reshape(x.shape[0] // 8, 8, x.shape[1]), axis=0)
        return sum(x[:, c : c + LANE] for c in range(0, x.shape[1], LANE))

    def alone(s, acc):
        rows = pl.ds(pl.multiple_of(s * 8, 8), 8)
        u, w = uc[rows, :], wb[pl.ds(pl.multiple_of(s * 8 + HB, 8), 8), LANE : LANE + W]
        before = uc[pl.ds(pl.multiple_of(jnp.maximum(s - 1, 0) * 8, 8), 8), :]
        after = uc[pl.ds(pl.multiple_of(jnp.minimum(s + 1, H // 8 - 1) * 8, 8), 8), :]
        before = jnp.where(s > 0, before, 0.0)
        after = jnp.where(s < H // 8 - 1, after, 0.0)
        beside = pltpu.roll(jnp.where(rows_w == 7, before, u), 1, 0)
        beside = beside + pltpu.roll(jnp.where(rows_w == 0, after, u), 7, 0)
        beside = beside + pltpu.roll(jnp.where(cols_w == W - 1, 0.0, u), 1, 1)
        beside = beside + pltpu.roll(jnp.where(cols_w == 0, 0.0, u), W - 1, 1)
        v = w * u + SMOOTH * (4.0 * u - beside)
        vc[rows, :] = v
        return acc[0] + u * u, acc[1] + u * v, acc[2] + v * v

    uu, uv, vv = lax.fori_loop(0, H // 8, alone, (jnp.zeros((8, W), F32),) * 3)

    def quotient(a, b):
        return jnp.where(b > 0.0, a / jnp.where(b > 0.0, b, 1.0), 0.0)

    near_step = quotient(total(fold(uv)), total(fold(vv)))

    def scale(s, _):
        rows = pl.ds(pl.multiple_of(s * 8, 8), 8)
        scaled[rows, :] = uc[rows, :] - near_step * vc[rows, :]
        return 0

    lax.fori_loop(0, H // 8, scale, 0)
    inner = W - 2 * LANE

    def curved(w, x, right, under):
        return w * (x * x) + SMOOTH * ((x - right) * (x - right) + (x - under) * (x - under))

    def middle(s, acc):
        row = pl.multiple_of(s * 8, 8)
        rows, there = pl.ds(row, 8), pl.ds(pl.multiple_of(s * 8 + HB, 8), 8)
        next_rows = pl.ds(pl.multiple_of(s * 8 + 8, 8), 8)
        u, w = uc[rows, LANE : W - LANE], wb[there, 2 * LANE : W]

        def parts(ref):
            x = ref[rows, LANE:W]
            right = pltpu.roll(x, inner + LANE - 1, 1)[:, 0:inner]
            x = x[:, 0:inner]
            under = pltpu.roll(jnp.where(rows_w[:, 0:inner] == 0, ref[next_rows, LANE : W - LANE], x), 7, 0)
            return x, x * x, curved(w, x, right, under)

        v, vv, vav = parts(vc)
        _, ss, sas = parts(scaled)
        return tuple(a + b for a, b in zip(acc, (u * v, vv, vav, ss, sas)))

    acc = lax.fori_loop(1, H // 8 - 1, middle, tuple(jnp.zeros((8, inner), F32) for _ in range(5)))
    tallies = [fold(uu)] + [fold(a) for a in acc]

    pl.semaphore_wait(chain.at[0], 2)
    entered(1)
    for c, _, recv_if in near:
        pl.when(recv_if)(c.wait_recv)

    pad = jnp.zeros((LANE - 8, LANE), F32)

    def there(x, present):
        return jnp.where(present, x, jnp.zeros_like(x))

    top = there(row_in[2], has_up)
    below, below_w = there(row_in[0], has_dn), there(row_in[1], has_dn)
    cols_rt = jnp.transpose(jnp.concatenate([there(col_in[0], has_rt), pad], axis=0))
    cols_rt_w = jnp.transpose(jnp.concatenate([there(col_in[1], has_rt), pad], axis=0))
    cols_lf = jnp.transpose(jnp.concatenate([pad, there(col_in[2], has_lf)], axis=0))
    corner_up = there(corner_in[0], has_up & has_rt)[7:8, :]
    corner_dn = there(corner_in[1], has_dn & has_rt)
    corner_lf = there(corner_in[2], has_dn & has_lf)
    tile_rows, tile_cols = iota((H, LANE), 0), iota((H, LANE), 1)
    for rows, cols, change in (
        (slice(0, 8), slice(0, W), jnp.where(rows_w == 0, pltpu.roll(top, 1, 0), 0.0)),
        (slice(H - 8, H), slice(0, W), jnp.where(rows_w == 7, pltpu.roll(below, 7, 0), 0.0)),
        (slice(0, H), slice(0, LANE), jnp.where(tile_cols == 0, pltpu.roll(cols_lf, 1, 1), 0.0)),
        (slice(0, H), slice(W - LANE, W), jnp.where(tile_cols == LANE - 1, pltpu.roll(cols_rt, LANE - 1, 1), 0.0)),
    ):
        vc[rows, cols] -= SMOOTH * change
        scaled[rows, cols] += near_step * (SMOOTH * change)

    beside = jnp.where(tile_rows == 0, corner_up, pltpu.roll(cols_rt, 1, 0))
    beside = beside + jnp.where(tile_rows == H - 1, corner_dn[0:1, :], pltpu.roll(cols_rt, H - 1, 0))
    beside = beside + pltpu.roll(uc[:, W - LANE : W], 1, 1) + pltpu.roll(cols_rt, LANE - 1, 1)
    v_rt = there(cols_rt_w * cols_rt + SMOOTH * (4.0 * cols_rt - beside), has_rt)

    line = jnp.concatenate([corner_lf, below, corner_dn], axis=1)
    beside = pltpu.roll(line, 1, 1)[:, LANE : LANE + W] + pltpu.roll(line, EW - 1, 1)[:, LANE : LANE + W]
    beside = beside + pltpu.roll(uc[H - 8 : H, :], 1, 0) + pltpu.roll(below, 7, 0)
    v_dn = there(below_w * below + SMOOTH * (4.0 * below - beside), has_dn)

    def shifted(x, beyond):
        x = jnp.concatenate([x, beyond], axis=1)
        return pltpu.roll(x, x.shape[1] - 1, 1)[:, 0 : x.shape[1] - LANE]

    body, body_next = slice(8, H - 8), slice(9, H - 7)
    first_cols, last_cols = slice(0, LANE), slice(W - LANE, W)

    def ring(ref, beyond, beneath):
        x = ref[0:8, :]
        yield x, shifted(x, beyond[0:8]), pltpu.roll(jnp.where(rows_w == 0, ref[8:16, :], x), 7, 0)
        x = ref[H - 8 : H, :]
        yield x, shifted(x, beyond[H - 8 : H]), pltpu.roll(jnp.where(rows_w == 0, beneath, x), 7, 0)
        x = ref[body, first_cols]
        yield x, shifted(x, ref[body, LANE : 2 * LANE]), ref[body_next, first_cols]
        x = ref[body, last_cols]
        yield x, shifted(x, beyond[8 : H - 8]), ref[body_next, last_cols]

    at_left = ((cols_w == 0) & (z == 0)).astype(F32)
    edges = (
        ((rows_w == 0) & (r == 0)).astype(F32) + at_left, at_left,
        ((iota((H - 16, LANE), 1) == 0) & (z == 0)).astype(F32), None,
    )
    areas = ((slice(0, 8), slice(0, W)), (slice(H - 8, H), slice(0, W)), (body, first_cols), (body, last_cols))
    s_rt, s_dn = cols_rt - near_step * v_rt, below - near_step * v_dn
    for (rows, cols), edge, of_v, of_s in zip(areas, edges, ring(vc, v_rt, v_dn), ring(scaled, s_rt, s_dn)):
        w = wb[rows.start + HB : rows.stop + HB, cols.start + LANE : cols.stop + LANE]
        w = w if edge is None else w + SMOOTH * edge
        v, s = of_v[0], of_s[0]
        new = (uc[rows, cols] * v, v * v, curved(w, *of_v), s * s, curved(w, *of_s))
        for k in range(5):
            tallies[k + 1] = tallies[k + 1] + fold(new[k])
    acc = tallies

    lane = iota((1, LANE), 1)
    packed = jnp.zeros((1, LANE), F32)
    for k, a in enumerate(acc):
        packed = jnp.where(lane == k, total(a), packed)
    packed = jnp.where((lane == 6) | (lane == 7), near_step, packed)
    msg[0] = packed

    def exchange(mine, slots, me, number, device, send_sem, recv_sem):
        copies = [
            pltpu.make_async_remote_copy(
                src_ref=mine, dst_ref=slots.at[me], send_sem=send_sem, recv_sem=recv_sem,
                device_id=device(lax.rem(me + k, number)), device_id_type=MESH,
            )
            for k in (PLANE_ORDER if number == ROWS else COLUMN_ORDER)
        ]
        for c in copies:
            c.start()
        slots[me] = mine[...]

    def settle(slots, number, sems):
        arrivals = slots.at[pl.ds(0, number - 1)]
        for sem in sems:
            pltpu.make_async_copy(arrivals, arrivals, sem).wait()

    exchange(msg.at[0], slots_p, r, ROWS, lambda i: (i, z), p_send, p_recv)

    for n in late:
        pl.when(wide[n][1])(wide[n][0].start)
    pl.semaphore_wait(chain.at[1], 2)
    entered(2)
    def square(height, width):
        return iota((height, width), 0), iota((height, width), 1)

    i, k = square(H, 256)
    at = r * H - REACH + k
    one = jnp.where((at >= 0) & (at < ROWS * H), tap(k - REACH - i), 0.0)
    k, j = square(256, 256)
    high, low = split(dot32(one, tap(k - j)))
    row_taps[0:H, :] = high
    row_taps[H : 2 * H, :] = low
    for n, t in enumerate((0, 3, 7)):
        j, k = square(256, 256)
        at = z * W + t * LANE - REACH + k
        one = jnp.where((at >= 0) & (at < COLS * W), tap(j - k), 0.0)
        k, i = square(256, LANE)
        high, low = split(dot32(one, tap(k - REACH - i)))
        col_taps[n, :, 0:LANE] = high
        col_taps[n, :, LANE : 2 * LANE] = low

    settle(slots_p, ROWS, (p_send, p_recv))

    def merge(slots, number, over):
        plain = jnp.sum(slots[...], axis=0)
        step = quotient(plain[:, over : over + 1], plain[:, over + 1 : over + 2])
        moved = jnp.zeros((1, LANE), F32)
        for n in range(number):
            x = slots[n]
            a, b, old = pltpu.roll(x, 3, 1), pltpu.roll(x, 2, 1), pltpu.roll(x, LANE - 2, 1)
            by = step - old
            moved = moved + (x - 2.0 * by * (a - old * b) + by * by * b)
        return jnp.where(lane < 4, plain, jnp.where(lane < 6, moved, step))

    msg[1] = merge(slots_p, ROWS, 1)
    pl.semaphore_wait(chain.at[2], 2)
    exchange(msg.at[1], slots_z, z, COLS, lambda i: (r, i), z_send, z_recv)

    for c, _, recv_if in wide:
        pl.when(recv_if)(c.wait_recv)

    def inside(row):
        at_row, at_col = rows8 + row + (r * H - HB), cols8 + z * W
        return (at_row >= 0) & (at_row < ROWS * H) & (at_col >= 0) & (at_col < COLS * W)

    def weighted(s, _):
        row = pl.multiple_of(s * 8, 8)
        here = pl.ds(row, 8)
        ub[here, :] = jnp.where(inside(row), fb[here, :] * wb[here, :], 0.0)
        return 0

    lax.fori_loop(0, BH // 8, weighted, 0)

    def extend(s, _):
        row = pl.multiple_of(s * 8 + 8, 8)
        here, there = pl.ds(row, 8), pl.ds(pl.multiple_of(s * 8, 8), 8)
        keep = inside(row)
        u = ub[here, :]
        v = jnp.where(keep, operator(ub, row, u, wb[here, :]), 0.0)
        f = jnp.where(keep, fb[here, :], 0.0)
        for dst, x in ((fx, f), (ux, u), (vx, v)):
            dst[there, :] = pltpu.roll(x, EW - (LANE - REACH), 1)[:, 0:SW]
        return 0

    lax.fori_loop(0, SH // 8, extend, 0)

    settle(slots_z, COLS, (z_send, z_recv))
    sums[...] = merge(slots_z, COLS, 0)

    for c, send_if, _ in near + wide:
        pl.when(send_if)(c.wait_send)


def blur_kernel(fx, ux, vx, uc, vc, row_taps, col_taps, sums, background, rms, field, scatter, sem):
    g = sums[...]
    uu, uau, vv, _, new, rar = (g[0:1, k : k + 1] for k in range(6))
    alpha = uu / uau
    beta = new / uu
    keep = 1.0 + beta
    curve = rar + 2.0 * beta * (uau - alpha * vv) + beta * beta * uau
    alpha1 = new / curve
    on_u = alpha + alpha1 * keep
    on_v = alpha1 * alpha
    field[...] = on_u * uc[...] - on_v * vc[...]
    writes = [pltpu.make_async_copy(field, background, sem.at[0])]
    writes[0].start()
    taps_hl, taps_h = row_taps[...], row_taps[0:H, :]
    wide = SW // 2
    parts = []
    for start in (0, wide // LANE * LANE, SW):
        parts.append(start)
    highs, lows = [], []
    for a, b in zip(parts[:-1], parts[1:]):
        s = fx[:, a:b] - (on_u * ux[:, a:b] - on_v * vx[:, a:b])
        high, low = split(s * s)
        both = jnp.dot(taps_hl, high, preferred_element_type=F32)
        y = both[0:H] + both[H : 2 * H] + jnp.dot(taps_h, low, preferred_element_type=F32)
        high, low = split(y)
        highs.append(high)
        lows.append(low)
    yh, yl = jnp.concatenate(highs, axis=1), jnp.concatenate(lows, axis=1)
    for t in range(W // LANE):
        n = 0 if t == 0 else 2 if t == W // LANE - 1 else 1
        window = slice(t * LANE, t * LANE + 256)
        both = jnp.dot(yh[:, window], col_taps[n], preferred_element_type=F32)
        out = both[:, 0:LANE] + both[:, LANE:]
        out = out + jnp.dot(yl[:, window], col_taps[n, :, 0:LANE], preferred_element_type=F32)
        scatter[:, t * LANE : (t + 1) * LANE] = jnp.sqrt(out + 1e-06)
        if t % 2:
            pair = pl.ds((t - 1) * LANE, 2 * LANE)
            writes.append(pltpu.make_async_copy(scatter.at[:, pair], rms.at[:, pair], sem.at[1 + t // 2]))
            writes[-1].start()
    for c in writes:
        c.wait()


def block(coadd_flux, inverse_variance, source_mask):
    vmem = pl.BlockSpec(memory_space=pltpu.VMEM)
    anywhere = pl.BlockSpec(memory_space=pltpu.HBM)
    fields = [jax.ShapeDtypeStruct((SH, SW), F32)] * 3 + [jax.ShapeDtypeStruct((H, W), F32)] * 2
    fields += [jax.ShapeDtypeStruct((2 * H, 256), BF16), jax.ShapeDtypeStruct((3, 256, 256), BF16)]
    fields += [jax.ShapeDtypeStruct((1, LANE), F32)]
    dma = pltpu.SemaphoreType.DMA
    mids = pl.pallas_call(
        gather_kernel,
        out_shape=fields,
        in_specs=[anywhere] * 3,
        out_specs=[vmem] * len(fields),
        scratch_shapes=[
            pltpu.VMEM((BH, EW), F32), pltpu.VMEM((BH, EW), F32), pltpu.VMEM((BH, EW), F32),
            pltpu.VMEM((H, W), F32), pltpu.VMEM((H, W), jnp.int32),
            pltpu.VMEM((H, W), F32), pltpu.VMEM((3, 8, W), F32), pltpu.VMEM((3, 8, LANE), F32),
            pltpu.VMEM((3, 8, LANE), F32), pltpu.VMEM((3, 8, LANE), F32),
            pltpu.VMEM((2, 1, LANE), F32), pltpu.VMEM((ROWS, 1, LANE), F32), pltpu.VMEM((COLS, 1, LANE), F32),
            dma((3,)), dma((9,)), dma((9,)), dma((16,)), dma((16,)), dma, dma, dma, dma, pltpu.SemaphoreType.REGULAR((3,)),
        ],
        compiler_params=pltpu.CompilerParams(collective_id=0, has_side_effects=True, vmem_limit_bytes=20 * 2**20),
        name="gather",
    )(*(pltpu.with_memory_space_constraint(x, pltpu.HBM) for x in (coadd_flux, inverse_variance, source_mask)))
    return pl.pallas_call(
        blur_kernel,
        out_shape=[jax.ShapeDtypeStruct((H, W), F32)] * 2,
        in_specs=[vmem] * len(fields),
        out_specs=[anywhere] * 2,
        scratch_shapes=[pltpu.VMEM((H, W), F32), pltpu.VMEM((H, W), F32), pltpu.SemaphoreType.DMA((1 + W // LANE // 2,))],
        compiler_params=pltpu.CompilerParams(vmem_limit_bytes=20 * 2**20),
        name="blur",
    )(*mids)


def solution(mesh):
    return jax.shard_map(
        block,
        mesh=mesh,
        in_specs=(P("rows", "cols"),) * 3,
        out_specs=(P("rows", "cols"),) * 2,
        check_vma=False,
    )
```

```python
import functools

import jax
import jax.numpy as jnp
import numpy as np
from jax import lax
from jax.experimental import pallas as pl
from jax.experimental.pallas import tpu as pltpu
from jax.sharding import PartitionSpec as P

RADIUS = 32
SIGMA = 10.0
SMOOTH = 2.0
REACH = 2 * RADIUS
ROWS, COLS = 32, 16
H, W = 128, 1024
HB = 72
LANE = 128
EW = W + 2 * LANE
BH = H + 2 * HB
SH, SW = H + 2 * REACH, W + 2 * REACH
MESH = pl.DeviceIdType.MESH
TAP_SUM = float(np.sum(np.exp(-np.arange(-RADIUS, RADIUS + 1) ** 2 / (2.0 * SIGMA * SIGMA))))
PLANE_ORDER = sorted(range(1, ROWS), key=lambda k: -min(k // 8, 4 - k // 8) - min(k % 8 // 2, 4 - k % 8 // 2))
COLUMN_ORDER = sorted(range(1, COLS), key=lambda k: -min(k, COLS - k))
F32 = jnp.float32
BF16 = jnp.bfloat16


def tap(distance):
    d = distance.astype(F32)
    value = jnp.exp(-d * d / (2.0 * SIGMA * SIGMA)) / TAP_SUM
    return jnp.where(jnp.abs(distance) <= RADIUS, value, 0.0)


def iota(shape, dim):
    return lax.broadcasted_iota(jnp.int32, shape, dim)


def split(x):
    high = x.astype(BF16)
    return high, (x - high.astype(F32)).astype(BF16)


def dot32(a, b):
    return jnp.dot(a, b, precision=lax.Precision.HIGHEST, preferred_element_type=F32)


def total(x):
    return jnp.sum(jnp.sum(x, axis=0, keepdims=True), axis=1, keepdims=True)


def gather_kernel(
    f_hbm, iv_hbm, mk_hbm,
    fx, ux, vx, uc, vc, row_taps, col_taps, sums,
    fb, wb, ub, ivb, mkb, scaled, row_in, corner_in, col_out, col_in, msg, slots_p, slots_z,
    load_sem, near_send, near_recv, wide_send, wide_recv, p_send, p_recv, z_send, z_recv, chain,
):
    r, z = lax.axis_index("rows"), lax.axis_index("cols")
    r_up, r_dn = lax.rem(r + ROWS - 1, ROWS), lax.rem(r + 1, ROWS)
    z_lf, z_rt = lax.rem(z + COLS - 1, COLS), lax.rem(z + 1, COLS)
    has_up, has_dn, has_lf, has_rt = r > 0, r < ROWS - 1, z > 0, z < COLS - 1

    loads = [
        pltpu.make_async_copy(f_hbm, fb.at[pl.ds(HB, H), pl.ds(LANE, W)], load_sem.at[0]),
        pltpu.make_async_copy(iv_hbm, ivb, load_sem.at[1]),
        pltpu.make_async_copy(mk_hbm, mkb, load_sem.at[2]),
    ]
    for c in loads:
        c.start()
    barrier = pltpu.get_barrier_semaphore()
    count = 0
    for a in (r_up, r_dn):
        for b in (z_lf, z_rt):
            pl.semaphore_signal(barrier, inc=1, device_id=(a, b), device_id_type=MESH)
            count += 1
    for k in PLANE_ORDER:
        pl.semaphore_signal(barrier, inc=1, device_id=(lax.rem(r + k, ROWS), z), device_id_type=MESH)
        count += 1
    for b in (z_lf, z_rt):
        pl.semaphore_signal(barrier, inc=1, device_id=(r, b), device_id_type=MESH)
        count += 1

    for c in loads:
        c.wait()

    def weigh(s, _):
        rows = pl.ds(pl.multiple_of(s * 8, 8), 8)
        there = pl.ds(pl.multiple_of(s * 8 + HB, 8), 8)
        w = ivb[rows, :] * (1.0 - mkb[rows, :].astype(F32))
        wb[there, LANE : LANE + W] = w
        uc[rows, :] = w * fb[there, LANE : LANE + W]
        return 0

    lax.fori_loop(0, H // 8, weigh, 0)
    col_out[0] = jnp.transpose(uc[:, 0:LANE])[0:8, :]
    col_out[1] = jnp.transpose(wb[HB : HB + H, LANE : 2 * LANE])[0:8, :]
    col_out[2] = jnp.transpose(uc[:, W - LANE : W])[LANE - 8 : LANE, :]

    pl.semaphore_wait(barrier, count)

    def entered(step):
        for away in (1 << step, COLS - (1 << step)):
            pl.semaphore_signal(chain.at[step], inc=1, device_id=(r, lax.rem(z + away, COLS)), device_id_type=MESH)

    entered(0)

    near = []

    def near_copy(src, dst, device, send_if, recv_if):
        k = len(near)
        c = pltpu.make_async_remote_copy(
            src_ref=src, dst_ref=dst, send_sem=near_send.at[k], recv_sem=near_recv.at[k],
            device_id=device, device_id_type=MESH,
        )
        near.append((c, send_if, recv_if))

    first, last = pl.ds(0, 8), pl.ds(H - 8, 8)
    mid, lf, rt = pl.ds(LANE, W), pl.ds(0, LANE), pl.ds(LANE + W, LANE)
    c_first, c_last = pl.ds(LANE, LANE), pl.ds(W, LANE)
    near_copy(uc.at[first], row_in.at[0], (r_up, z), has_up, has_dn)
    near_copy(wb.at[pl.ds(HB, 8), mid], row_in.at[1], (r_up, z), has_up, has_dn)
    near_copy(uc.at[last], row_in.at[2], (r_dn, z), has_dn, has_up)
    near_copy(col_out.at[0], col_in.at[0], (r, z_lf), has_lf, has_rt)
    near_copy(col_out.at[1], col_in.at[1], (r, z_lf), has_lf, has_rt)
    near_copy(col_out.at[2], col_in.at[2], (r, z_rt), has_rt, has_lf)
    block_lf, block_rt = pl.ds(0, LANE), pl.ds(W - LANE, LANE)
    near_copy(uc.at[last, block_lf], corner_in.at[0], (r_dn, z_lf), has_dn & has_lf, has_up & has_rt)
    near_copy(uc.at[first, block_lf], corner_in.at[1], (r_up, z_lf), has_up & has_lf, has_dn & has_rt)
    near_copy(uc.at[first, block_rt], corner_in.at[2], (r_up, z_rt), has_up & has_rt, has_dn & has_lf)
    for c, send_if, _ in near:
        pl.when(send_if)(c.start)
    wide = []

    def wide_copy(src_rows, src_cols, dst_rows, dst_cols, device, send_if, recv_if):
        for buf in (fb, wb):
            k = len(wide)
            c = pltpu.make_async_remote_copy(
                src_ref=buf.at[src_rows, src_cols], dst_ref=buf.at[dst_rows, dst_cols],
                send_sem=wide_send.at[k], recv_sem=wide_recv.at[k], device_id=device, device_id_type=MESH,
            )
            wide.append((c, send_if, recv_if))

    w_first, w_last, every = pl.ds(HB, HB), pl.ds(H, HB), pl.ds(HB, H)
    w_top, w_below = pl.ds(0, HB), pl.ds(HB + H, HB)
    wide_copy(every, c_first, every, rt, (r, z_lf), has_lf, has_rt)
    wide_copy(every, c_last, every, lf, (r, z_rt), has_rt, has_lf)
    wide_copy(w_first, mid, w_below, mid, (r_up, z), has_up, has_dn)
    wide_copy(w_last, mid, w_top, mid, (r_dn, z), has_dn, has_up)
    wide_copy(w_first, c_first, w_below, rt, (r_up, z_lf), has_up & has_lf, has_dn & has_rt)
    wide_copy(w_first, c_last, w_below, lf, (r_up, z_rt), has_up & has_rt, has_dn & has_lf)
    wide_copy(w_last, c_first, w_top, rt, (r_dn, z_lf), has_dn & has_lf, has_up & has_rt)
    wide_copy(w_last, c_last, w_top, lf, (r_dn, z_rt), has_dn & has_rt, has_up & has_lf)
    early = [n for n in range(len(wide)) if n not in (5, 7)]
    late = [5, 7]
    for n in early:
        pl.when(wide[n][1])(wide[n][0].start)

    cols8 = iota((8, EW), 1) - LANE
    rows8 = iota((8, EW), 0)

    def higher(src, row, x):
        before = src[pl.ds(pl.multiple_of(row - 8, 8), 8), :]
        return pltpu.roll(jnp.where(rows8 == 7, before, x), 1, 0)

    def lower(src, row, x):
        after = src[pl.ds(pl.multiple_of(row + 8, 8), 8), :]
        return pltpu.roll(jnp.where(rows8 == 0, after, x), 7, 0)

    def operator(src, row, u, w):
        above, under = higher(src, row, u), lower(src, row, u)
        beside = above + under + pltpu.roll(u, 1, 1) + pltpu.roll(u, EW - 1, 1)
        return w * u + SMOOTH * (4.0 * u - beside)

    rows_w, cols_w = iota((8, W), 0), iota((8, W), 1)
    lanes8 = iota((8, LANE), 1)

    def fold(x):
        x = jnp.sum(x.reshape(x.shape[0] // 8, 8, x.shape[1]), axis=0)
        return sum(x[:, c : c + LANE] for c in range(0, x.shape[1], LANE))

    def alone(s, acc):
        rows = pl.ds(pl.multiple_of(s * 8, 8), 8)
        u, w = uc[rows, :], wb[pl.ds(pl.multiple_of(s * 8 + HB, 8), 8), LANE : LANE + W]
        before = uc[pl.ds(pl.multiple_of(jnp.maximum(s - 1, 0) * 8, 8), 8), :]
        after = uc[pl.ds(pl.multiple_of(jnp.minimum(s + 1, H // 8 - 1) * 8, 8), 8), :]
        before = jnp.where(s > 0, before, 0.0)
        after = jnp.where(s < H // 8 - 1, after, 0.0)
        beside = pltpu.roll(jnp.where(rows_w == 7, before, u), 1, 0)
        beside = beside + pltpu.roll(jnp.where(rows_w == 0, after, u), 7, 0)
        beside = beside + pltpu.roll(jnp.where(cols_w == W - 1, 0.0, u), 1, 1)
        beside = beside + pltpu.roll(jnp.where(cols_w == 0, 0.0, u), W - 1, 1)
        v = w * u + SMOOTH * (4.0 * u - beside)
        vc[rows, :] = v
        return acc[0] + u * u, acc[1] + u * v, acc[2] + v * v

    uu, uv, vv = lax.fori_loop(0, H // 8, alone, (jnp.zeros((8, W), F32),) * 3)

    def quotient(a, b):
        return jnp.where(b > 0.0, a / jnp.where(b > 0.0, b, 1.0), 0.0)

    near_step = quotient(total(fold(uv)), total(fold(vv)))

    def scale(s, _):
        rows = pl.ds(pl.multiple_of(s * 8, 8), 8)
        scaled[rows, :] = uc[rows, :] - near_step * vc[rows, :]
        return 0

    lax.fori_loop(0, H // 8, scale, 0)
    inner = W - 2 * LANE

    pl.semaphore_wait(chain.at[0], 2)
    entered(1)

    def curved(w, x, right, under):
        return w * (x * x) + SMOOTH * ((x - right) * (x - right) + (x - under) * (x - under))

    def middle(s, acc):
        row = pl.multiple_of(s * 8, 8)
        rows, there = pl.ds(row, 8), pl.ds(pl.multiple_of(s * 8 + HB, 8), 8)
        next_rows = pl.ds(pl.multiple_of(s * 8 + 8, 8), 8)
        u, w = uc[rows, LANE : W - LANE], wb[there, 2 * LANE : W]

        def parts(ref):
            x = ref[rows, LANE:W]
            right = pltpu.roll(x, inner + LANE - 1, 1)[:, 0:inner]
            x = x[:, 0:inner]
            under = pltpu.roll(jnp.where(rows_w[:, 0:inner] == 0, ref[next_rows, LANE : W - LANE], x), 7, 0)
            return x, x * x, curved(w, x, right, under)

        v, vv, vav = parts(vc)
        _, ss, sas = parts(scaled)
        return tuple(a + b for a, b in zip(acc, (u * v, vv, vav, ss, sas)))

    acc = lax.fori_loop(1, H // 8 - 1, middle, tuple(jnp.zeros((8, inner), F32) for _ in range(5)))
    tallies = [fold(uu)] + [fold(a) for a in acc]

    for c, _, recv_if in near:
        pl.when(recv_if)(c.wait_recv)

    pad = jnp.zeros((LANE - 8, LANE), F32)

    def there(x, present):
        return jnp.where(present, x, jnp.zeros_like(x))

    top = there(row_in[2], has_up)
    below, below_w = there(row_in[0], has_dn), there(row_in[1], has_dn)
    cols_rt = jnp.transpose(jnp.concatenate([there(col_in[0], has_rt), pad], axis=0))
    cols_rt_w = jnp.transpose(jnp.concatenate([there(col_in[1], has_rt), pad], axis=0))
    cols_lf = jnp.transpose(jnp.concatenate([pad, there(col_in[2], has_lf)], axis=0))
    corner_up = there(corner_in[0], has_up & has_rt)[7:8, :]
    corner_dn = there(corner_in[1], has_dn & has_rt)
    corner_lf = there(corner_in[2], has_dn & has_lf)
    tile_rows, tile_cols = iota((H, LANE), 0), iota((H, LANE), 1)
    for rows, cols, change in (
        (slice(0, 8), slice(0, W), jnp.where(rows_w == 0, pltpu.roll(top, 1, 0), 0.0)),
        (slice(H - 8, H), slice(0, W), jnp.where(rows_w == 7, pltpu.roll(below, 7, 0), 0.0)),
        (slice(0, H), slice(0, LANE), jnp.where(tile_cols == 0, pltpu.roll(cols_lf, 1, 1), 0.0)),
        (slice(0, H), slice(W - LANE, W), jnp.where(tile_cols == LANE - 1, pltpu.roll(cols_rt, LANE - 1, 1), 0.0)),
    ):
        vc[rows, cols] -= SMOOTH * change
        scaled[rows, cols] += near_step * (SMOOTH * change)

    beside = jnp.where(tile_rows == 0, corner_up, pltpu.roll(cols_rt, 1, 0))
    beside = beside + jnp.where(tile_rows == H - 1, corner_dn[0:1, :], pltpu.roll(cols_rt, H - 1, 0))
    beside = beside + pltpu.roll(uc[:, W - LANE : W], 1, 1) + pltpu.roll(cols_rt, LANE - 1, 1)
    v_rt = there(cols_rt_w * cols_rt + SMOOTH * (4.0 * cols_rt - beside), has_rt)

    line = jnp.concatenate([corner_lf, below, corner_dn], axis=1)
    beside = pltpu.roll(line, 1, 1)[:, LANE : LANE + W] + pltpu.roll(line, EW - 1, 1)[:, LANE : LANE + W]
    beside = beside + pltpu.roll(uc[H - 8 : H, :], 1, 0) + pltpu.roll(below, 7, 0)
    v_dn = there(below_w * below + SMOOTH * (4.0 * below - beside), has_dn)

    def shifted(x, beyond):
        x = jnp.concatenate([x, beyond], axis=1)
        return pltpu.roll(x, x.shape[1] - 1, 1)[:, 0 : x.shape[1] - LANE]

    body, body_next = slice(8, H - 8), slice(9, H - 7)
    first_cols, last_cols = slice(0, LANE), slice(W - LANE, W)

    def ring(ref, beyond, beneath):
        x = ref[0:8, :]
        yield x, shifted(x, beyond[0:8]), pltpu.roll(jnp.where(rows_w == 0, ref[8:16, :], x), 7, 0)
        x = ref[H - 8 : H, :]
        yield x, shifted(x, beyond[H - 8 : H]), pltpu.roll(jnp.where(rows_w == 0, beneath, x), 7, 0)
        x = ref[body, first_cols]
        yield x, shifted(x, ref[body, LANE : 2 * LANE]), ref[body_next, first_cols]
        x = ref[body, last_cols]
        yield x, shifted(x, beyond[8 : H - 8]), ref[body_next, last_cols]

    at_left = ((cols_w == 0) & (z == 0)).astype(F32)
    edges = (
        ((rows_w == 0) & (r == 0)).astype(F32) + at_left, at_left,
        ((iota((H - 16, LANE), 1) == 0) & (z == 0)).astype(F32), None,
    )
    areas = ((slice(0, 8), slice(0, W)), (slice(H - 8, H), slice(0, W)), (body, first_cols), (body, last_cols))
    s_rt, s_dn = cols_rt - near_step * v_rt, below - near_step * v_dn
    for (rows, cols), edge, of_v, of_s in zip(areas, edges, ring(vc, v_rt, v_dn), ring(scaled, s_rt, s_dn)):
        w = wb[rows.start + HB : rows.stop + HB, cols.start + LANE : cols.stop + LANE]
        w = w if edge is None else w + SMOOTH * edge
        v, s = of_v[0], of_s[0]
        new = (uc[rows, cols] * v, v * v, curved(w, *of_v), s * s, curved(w, *of_s))
        for k in range(5):
            tallies[k + 1] = tallies[k + 1] + fold(new[k])
    acc = tallies

    lane = iota((1, LANE), 1)
    packed = jnp.zeros((1, LANE), F32)
    for k, a in enumerate(acc):
        packed = jnp.where(lane == k, total(a), packed)
    packed = jnp.where((lane == 6) | (lane == 7), near_step, packed)
    msg[0] = packed

    def exchange(mine, slots, me, number, device, send_sem, recv_sem):
        copies = [
            pltpu.make_async_remote_copy(
                src_ref=mine, dst_ref=slots.at[me], send_sem=send_sem, recv_sem=recv_sem,
                device_id=device(lax.rem(me + k, number)), device_id_type=MESH,
            )
            for k in (PLANE_ORDER if number == ROWS else COLUMN_ORDER)
        ]
        for c in copies:
            c.start()
        slots[me] = mine[...]

    def settle(slots, number, sems):
        arrivals = slots.at[pl.ds(0, number - 1)]
        for sem in sems:
            pltpu.make_async_copy(arrivals, arrivals, sem).wait()

    exchange(msg.at[0], slots_p, r, ROWS, lambda i: (i, z), p_send, p_recv)

    for n in late:
        pl.when(wide[n][1])(wide[n][0].start)
    pl.semaphore_wait(chain.at[1], 2)
    entered(2)
    def square(height, width):
        return iota((height, width), 0), iota((height, width), 1)

    i, k = square(H, 256)
    at = r * H - REACH + k
    one = jnp.where((at >= 0) & (at < ROWS * H), tap(k - REACH - i), 0.0)
    k, j = square(256, 256)
    high, low = split(dot32(one, tap(k - j)))
    row_taps[0:H, :] = high
    row_taps[H : 2 * H, :] = low
    for n, t in enumerate((0, 3, 7)):
        j, k = square(256, 256)
        at = z * W + t * LANE - REACH + k
        one = jnp.where((at >= 0) & (at < COLS * W), tap(j - k), 0.0)
        k, i = square(256, LANE)
        high, low = split(dot32(one, tap(k - REACH - i)))
        col_taps[n, :, 0:LANE] = high
        col_taps[n, :, LANE : 2 * LANE] = low

    settle(slots_p, ROWS, (p_send, p_recv))

    def merge(slots, number, over):
        x = slots[...].reshape(number, LANE)
        plain = jnp.sum(x, axis=0, keepdims=True)
        step = quotient(plain[:, over : over + 1], plain[:, over + 1 : over + 2])
        a, b, old = pltpu.roll(x, 3, 1), pltpu.roll(x, 2, 1), pltpu.roll(x, LANE - 2, 1)
        by = step - old
        moved = jnp.sum(x - 2.0 * by * (a - old * b) + by * by * b, axis=0, keepdims=True)
        return jnp.where(lane < 4, plain, jnp.where(lane < 6, moved, step))

    msg[1] = merge(slots_p, ROWS, 1)
    pl.semaphore_wait(chain.at[2], 2)
    exchange(msg.at[1], slots_z, z, COLS, lambda i: (r, i), z_send, z_recv)

    for c, _, recv_if in wide:
        pl.when(recv_if)(c.wait_recv)

    def inside(row):
        at_row, at_col = rows8 + row + (r * H - HB), cols8 + z * W
        return (at_row >= 0) & (at_row < ROWS * H) & (at_col >= 0) & (at_col < COLS * W)

    def weighted(s, _):
        row = pl.multiple_of(s * 8, 8)
        here = pl.ds(row, 8)
        ub[here, :] = jnp.where(inside(row), fb[here, :] * wb[here, :], 0.0)
        return 0

    lax.fori_loop(0, BH // 8, weighted, 0)

    def extend(s, _):
        row = pl.multiple_of(s * 8 + 8, 8)
        here, there = pl.ds(row, 8), pl.ds(pl.multiple_of(s * 8, 8), 8)
        keep = inside(row)
        u = ub[here, :]
        v = jnp.where(keep, operator(ub, row, u, wb[here, :]), 0.0)
        f = jnp.where(keep, fb[here, :], 0.0)
        for dst, x in ((fx, f), (ux, u), (vx, v)):
            dst[there, :] = pltpu.roll(x, EW - (LANE - REACH), 1)[:, 0:SW]
        return 0

    lax.fori_loop(0, SH // 8, extend, 0)

    settle(slots_z, COLS, (z_send, z_recv))
    sums[...] = merge(slots_z, COLS, 0)

    for c, send_if, _ in near + wide:
        pl.when(send_if)(c.wait_send)


def blur_kernel(fx, ux, vx, uc, vc, row_taps, col_taps, sums, background, rms, field, scatter, sem):
    g = sums[...]
    uu, uau, vv, _, new, rar = (g[0:1, k : k + 1] for k in range(6))
    alpha = uu / uau
    beta = new / uu
    keep = 1.0 + beta
    curve = rar + 2.0 * beta * (uau - alpha * vv) + beta * beta * uau
    alpha1 = new / curve
    on_u = alpha + alpha1 * keep
    on_v = alpha1 * alpha
    field[...] = on_u * uc[...] - on_v * vc[...]
    writes = [pltpu.make_async_copy(field, background, sem.at[0])]
    writes[0].start()
    taps_hl, taps_h = row_taps[...], row_taps[0:H, :]
    wide = SW // 2
    parts = []
    for start in (0, wide // LANE * LANE, SW):
        parts.append(start)
    highs, lows = [], []
    for a, b in zip(parts[:-1], parts[1:]):
        s = fx[:, a:b] - (on_u * ux[:, a:b] - on_v * vx[:, a:b])
        high, low = split(s * s)
        both = jnp.dot(taps_hl, high, preferred_element_type=F32)
        y = both[0:H] + both[H : 2 * H] + jnp.dot(taps_h, low, preferred_element_type=F32)
        high, low = split(y)
        highs.append(high)
        lows.append(low)
    yh, yl = jnp.concatenate(highs, axis=1), jnp.concatenate(lows, axis=1)
    for t in range(W // LANE):
        n = 0 if t == 0 else 2 if t == W // LANE - 1 else 1
        window = slice(t * LANE, t * LANE + 256)
        both = jnp.dot(yh[:, window], col_taps[n], preferred_element_type=F32)
        out = both[:, 0:LANE] + both[:, LANE:]
        out = out + jnp.dot(yl[:, window], col_taps[n, :, 0:LANE], preferred_element_type=F32)
        scatter[:, t * LANE : (t + 1) * LANE] = jnp.sqrt(out + 1e-06)
        if t % 2:
            pair = pl.ds((t - 1) * LANE, 2 * LANE)
            writes.append(pltpu.make_async_copy(scatter.at[:, pair], rms.at[:, pair], sem.at[1 + t // 2]))
            writes[-1].start()
    for c in writes:
        c.wait()


def block(coadd_flux, inverse_variance, source_mask):
    vmem = pl.BlockSpec(memory_space=pltpu.VMEM)
    anywhere = pl.BlockSpec(memory_space=pltpu.HBM)
    fields = [jax.ShapeDtypeStruct((SH, SW), F32)] * 3 + [jax.ShapeDtypeStruct((H, W), F32)] * 2
    fields += [jax.ShapeDtypeStruct((2 * H, 256), BF16), jax.ShapeDtypeStruct((3, 256, 256), BF16)]
    fields += [jax.ShapeDtypeStruct((1, LANE), F32)]
    dma = pltpu.SemaphoreType.DMA
    mids = pl.pallas_call(
        gather_kernel,
        out_shape=fields,
        in_specs=[anywhere] * 3,
        out_specs=[vmem] * len(fields),
        scratch_shapes=[
            pltpu.VMEM((BH, EW), F32), pltpu.VMEM((BH, EW), F32), pltpu.VMEM((BH, EW), F32),
            pltpu.VMEM((H, W), F32), pltpu.VMEM((H, W), jnp.int32),
            pltpu.VMEM((H, W), F32), pltpu.VMEM((3, 8, W), F32), pltpu.VMEM((3, 8, LANE), F32),
            pltpu.VMEM((3, 8, LANE), F32), pltpu.VMEM((3, 8, LANE), F32),
            pltpu.VMEM((2, 1, LANE), F32), pltpu.VMEM((ROWS, 1, LANE), F32), pltpu.VMEM((COLS, 1, LANE), F32),
            dma((3,)), dma((9,)), dma((9,)), dma((16,)), dma((16,)), dma, dma, dma, dma, pltpu.SemaphoreType.REGULAR((3,)),
        ],
        compiler_params=pltpu.CompilerParams(collective_id=0, has_side_effects=True, vmem_limit_bytes=20 * 2**20),
        name="gather",
    )(*(pltpu.with_memory_space_constraint(x, pltpu.HBM) for x in (coadd_flux, inverse_variance, source_mask)))
    return pl.pallas_call(
        blur_kernel,
        out_shape=[jax.ShapeDtypeStruct((H, W), F32)] * 2,
        in_specs=[vmem] * len(fields),
        out_specs=[anywhere] * 2,
        scratch_shapes=[pltpu.VMEM((H, W), F32), pltpu.VMEM((H, W), F32), pltpu.SemaphoreType.DMA((1 + W // LANE // 2,))],
        compiler_params=pltpu.CompilerParams(vmem_limit_bytes=20 * 2**20),
        name="blur",
    )(*mids)


def solution(mesh):
    return jax.shard_map(
        block,
        mesh=mesh,
        in_specs=(P("rows", "cols"),) * 3,
        out_specs=(P("rows", "cols"),) * 2,
        check_vma=False,
    )
```
